512 devices in a mesh: seq: 16 (over z), wide: 8 (over x, y_hi), narrow: 4 (over y_lo, core).
Axes of the slice: x: 4, y: 4 (y_hi: 2, y_lo: 2; y = y_hi * 2 + y_lo), z: 16, core: 2. Of those that a mesh axis runs over, the one named last changes fastest.
Arguments:
- tokens: bfloat16 [8192, 4096], P('seq', 'narrow'), may hold values from -6 to 6
- norm_gain: float32 [4096], P('narrow'), may hold values from 0.25 to 1.75
- q_weight: bfloat16 [4096, 4096], P('narrow', 'wide'), may hold values from -1 to 1
- kv_weight: bfloat16 [4096, 1024], P('narrow', 'wide'), may hold values from -1 to 1
- out_weight: bfloat16 [4096, 4096], P('wide', 'narrow'), may hold values from -0.09375 to 0.09375
- lengths: int32 [4], replicated, may hold values from 1 to 4096, as said below
- page_table: int32 [256], replicated, may hold values from 0 to 255, as said below
Outputs:
- hidden: bfloat16 [8192, 4096], P(('seq', 'wide'), 'narrow')
- kv_cache: bfloat16 [256, 32, 1024], P('seq', None, 'wide')
The draws below stay inside these ranges and needn't reach their ends.
Inputs may be any that keep to these rules, and one draw needn't show every extreme that they name: Prompts lie end to end in the stream in the order given; their lengths sum to 8192, and exactly one prompt has 4096 tokens. `page_table`: the entries are a permutation. Entry s * 16 + j is the slot of page j of the s-th block of 512 tokens; slot r * 16 + i belongs to the r-th index of seq, and the 16 pages of one block belong to 16 different indices of seq.
All inputs are finite; a program needn't handle non-finite values.
Results may differ from the reference program's by a relative error of at most 0.008.
Values may be sent and summed in bfloat16 or wider, within the bound.
A program may use at most 64 MiB of HBM per device.

```python
import jax
import jax.numpy as jnp
from jax import lax

D = 4096
HEADS = 32
KV_HEADS = 4
HD = 128
TOK_DEV = 512
PROMPTS = 4
TOKENS = 8192
MAXLEN = 4096
PEERS = 16
PAGE = 32
SLOTS = 256
QW = 4096
KVW = 1024
N_SEQ = 16


def base_weight(key, columns):
    noise = jax.random.normal(key, (D, columns), jnp.float32)
    return jnp.clip(noise, -3.0, 3.0) / D ** 0.5


def prompt_lengths(key):
    keys = jax.random.split(jax.random.fold_in(key, 3), PROMPTS + 2)
    where_long = jax.random.randint(keys[0], (), 1, PROMPTS - 1).astype(jnp.int32)
    after_count = PROMPTS - 1 - where_long
    lead = jax.random.randint(keys[1], (), where_long, MAXLEN - after_count + 1).astype(jnp.int32)
    lead = (lead + (lead % TOK_DEV == 0).astype(jnp.int32)).astype(jnp.int32)
    rem_before = lead
    rem_after = (MAXLEN - lead).astype(jnp.int32)
    pieces = []
    for number in range(PROMPTS):
        in_before = number < where_long
        left = jnp.where(in_before, where_long - 1 - number, PROMPTS - 1 - number).astype(jnp.int32)
        remain = jnp.where(in_before, rem_before, rem_after).astype(jnp.int32)
        upper = jnp.maximum(remain - left + 1, 2)
        drawn = jax.random.randint(keys[2 + number], (), 1, upper).astype(jnp.int32)
        piece = jnp.where(left == 0, remain, drawn)
        piece = jnp.where(number == where_long, MAXLEN, piece).astype(jnp.int32)
        rem_before = jnp.where(in_before, rem_before - piece, rem_before).astype(jnp.int32)
        rem_after = jnp.where(number > where_long, rem_after - piece, rem_after).astype(jnp.int32)
        pieces.append(piece)
    return jnp.stack(pieces).astype(jnp.int32)


def draw_lengths(key, part):
    return prompt_lengths(key)


def draw_tokens(key, part):
    noise_key = jax.random.fold_in(jax.random.fold_in(key, 21), 0)
    drawn = jnp.clip(jax.random.normal(noise_key, (TOKENS, D), jnp.float32), -6.0, 6.0)
    return drawn.astype(jnp.bfloat16)


def draw_q_weight(key, part):
    drawn = base_weight(jax.random.fold_in(key, 31), QW)
    return drawn.astype(jnp.bfloat16)


def draw_kv_weight(key, part):
    drawn = base_weight(jax.random.fold_in(key, 41), KVW)
    return drawn.astype(jnp.bfloat16)


def draw_page_table(key, part):
    first_key, second_key = jax.random.split(jax.random.fold_in(key, 7))
    base = jnp.tile(jnp.arange(PEERS, dtype=jnp.int32)[None, :], (PEERS, 1))
    owners = jax.random.permutation(first_key, base, axis=1, independent=True)
    spots = jax.random.permutation(second_key, base, axis=1, independent=True)
    source = jnp.broadcast_to(jnp.arange(PEERS, dtype=jnp.int32)[:, None], (PEERS, PEERS))
    slot = owners * PEERS + spots[owners, source]
    return slot.reshape(PEERS * PEERS).astype(jnp.int32)


def steps_of(key, dims, cuts, low, largest):
    def one(axis_at, shards_of):
        heights = jax.random.uniform(jax.random.fold_in(jax.random.fold_in(key, 6), axis_at), (shards_of,), jnp.float32, low / len(cuts), largest / len(cuts))
        return jnp.repeat(jnp.exp(heights), dims[axis_at] // shards_of).reshape((-1,) + (1,) * (len(dims) - axis_at - 1))

    factor_of = one(*cuts[0])
    for cut in cuts[1:]:
        factor_of = factor_of * one(*cut)
    return factor_of


def normal_values(key, shape, deviation, bound, shards=(), held_as=jnp.bfloat16):
    array = jax.random.normal(key, shape, jnp.float32) * deviation
    if len(shards) > 0:
        array = steps_of(key, shape, shards, -0.22, 0.18) * array
    return jnp.clip(array, min=-bound, max=bound).astype(held_as)


def setup_inputs(seed: int = 0) -> dict:
    key_list = jax.random.split(jax.random.key(seed), 8)
    return {
        "tokens": draw_tokens(jax.random.fold_in(key_list[7], 71), 0),
        "norm_gain": jnp.clip(1.0 + 0.15 * jax.random.normal(key_list[1], (D,), jnp.float32), 0.25, 1.75),
        "q_weight": draw_q_weight(jax.random.fold_in(key_list[7], 71), 0),
        "kv_weight": draw_kv_weight(jax.random.fold_in(key_list[7], 71), 0),
        "out_weight": normal_values(key_list[4], (QW, D), QW ** -0.5, 0.09375, ((0, 8), (1, 4))),
        "lengths": draw_lengths(jax.random.fold_in(key_list[7], 71), 0),
        "page_table": draw_page_table(jax.random.fold_in(key_list[7], 71), 0),
    }


EPS = 1e-05
THETA = 5000000.0

def prompt_index(lengths, index):
    ends = jnp.cumsum(lengths).astype(jnp.int32)
    starts = ends - lengths
    segment = lax.optimization_barrier(jnp.sum((index[:, None] >= ends[None, :]).astype(jnp.int32), axis=1))
    onehot = segment[:, None] == jnp.arange(lengths.shape[0], dtype=jnp.int32)[None, :]
    begin = lax.optimization_barrier(jnp.sum(jnp.where(onehot, starts[None, :], 0), axis=1)).astype(jnp.int32)
    return (segment, index - begin)

def rotate(values, position, head_dim):
    rows = values.shape[0]
    heads = values.shape[1] // head_dim
    half = head_dim // 2
    freq = THETA ** (-jnp.arange(half, dtype=jnp.float32) * 2.0 / head_dim)
    angle = position.astype(jnp.float32)[:, None] * freq[None, :]
    cosine = jnp.cos(angle)[:, None, :]
    sine = jnp.sin(angle)[:, None, :]
    shaped = values.reshape(rows, heads, head_dim)
    first = shaped[..., :half]
    second = shaped[..., half:]
    turned = jnp.concatenate([first * cosine - second * sine, second * cosine + first * sine], axis=-1)
    return turned.reshape(rows, heads * head_dim)

def reference(tokens, norm_gain, q_weight, kv_weight, out_weight, lengths, page_table):
    count = tokens.shape[0]
    index = jnp.arange(count, dtype=jnp.int32)
    segment, position = prompt_index(lengths, index)
    wide_x = tokens.astype(jnp.float32)
    rinv = lax.rsqrt(lax.optimization_barrier(jnp.sum(wide_x * wide_x, axis=1)) / D + EPS)
    scaled = (wide_x * norm_gain[None, :]).astype(jnp.bfloat16)
    queries = jnp.dot(scaled, q_weight, preferred_element_type=jnp.float32) * rinv[:, None]
    queries = rotate(queries, position, HD).astype(jnp.bfloat16)
    kv_full = jnp.dot(scaled, kv_weight, preferred_element_type=jnp.float32) * rinv[:, None]
    keys = rotate(kv_full[:, :KV_HEADS * HD], position, HD).astype(jnp.bfloat16)
    values = kv_full[:, KV_HEADS * HD:].astype(jnp.bfloat16)
    group = HEADS // KV_HEADS
    keys_f = keys.astype(jnp.float32).reshape(count, KV_HEADS, HD)
    values_f = values.astype(jnp.float32).reshape(count, KV_HEADS, HD)
    span = min(count, (N_SEQ // 2 + 1) * TOK_DEV)
    scale = 1.0 / HD ** 0.5

    def attend(block):
        start = (block * TOK_DEV).astype(jnp.int32)
        k_start = jnp.maximum(start + TOK_DEV - span, 0).astype(jnp.int32)
        qrows = lax.dynamic_slice_in_dim(queries, start, TOK_DEV, 0).astype(jnp.float32)
        qrows = qrows.reshape(TOK_DEV, KV_HEADS, group, HD)
        krows = lax.dynamic_slice_in_dim(keys_f, k_start, span, 0)
        vrows = lax.dynamic_slice_in_dim(values_f, k_start, span, 0)
        q_seg = lax.dynamic_slice_in_dim(segment, start, TOK_DEV, 0)
        k_seg = lax.dynamic_slice_in_dim(segment, k_start, span, 0)
        q_idx = start + jnp.arange(TOK_DEV, dtype=jnp.int32)
        k_idx = k_start + jnp.arange(span, dtype=jnp.int32)
        allowed = (k_seg[None, :] == q_seg[:, None]) & (k_idx[None, :] <= q_idx[:, None])
        scores = jnp.einsum('qkgd,skd->kgqs', qrows, krows) * scale
        masked = jnp.where(allowed[None, None], scores, -1e+30)
        top = lax.optimization_barrier(jnp.max(masked, axis=-1))
        weights = jnp.where(allowed[None, None], jnp.exp(masked - top[..., None]), 0.0)
        total = lax.optimization_barrier(jnp.sum(weights, axis=-1))
        rounded = weights.astype(jnp.bfloat16).astype(jnp.float32)
        mixed = jnp.einsum('kgqs,skd->qkgd', rounded, vrows)
        mixed = mixed / jnp.transpose(total, (2, 0, 1))[..., None]
        return mixed.reshape(TOK_DEV, HEADS * HD).astype(jnp.bfloat16)
    attended = lax.map(attend, jnp.arange(N_SEQ, dtype=jnp.int32)).reshape(count, HEADS * HD)
    projected = jnp.dot(attended, out_weight, preferred_element_type=jnp.float32)
    hidden = (wide_x + projected).astype(jnp.bfloat16)
    kv_all = jnp.concatenate([keys, values], axis=1)
    pages = kv_all.reshape(count // PAGE, PAGE, 2 * KV_HEADS * HD)
    cache = jnp.zeros((SLOTS, PAGE, 2 * KV_HEADS * HD), jnp.bfloat16).at[page_table].set(pages)
    return (hidden, cache)
```

```python
import jax
import jax.numpy as jnp
import numpy as np
from jax import lax
from jax.experimental import pallas as pl
from jax.experimental.pallas import tpu as pltpu
from jax.sharding import PartitionSpec as P

HEADS = 32
KV_HEADS = 4
HD = 128
WIDTH = 4096
BLOCK = 512
QUARTER = 128
EPS = 1e-05
THETA = 5000000.0
NEG = -1e30
BACK = 8
MESH = pl.DeviceIdType.MESH
F32 = jnp.float32
BF16 = jnp.bfloat16


def kernel(
    lens, table, gain, freq, tok_any, kvw_any, qw_any, ow_any,
    hid, cache,
    tok, kvw, qw, ow, scaled, kvp, kvr, qf, qs1, qr1, qs2, qr2, mykv,
    kv_all, queries, m_s, l_s, acc_s, cos_s, sin_s, rinv_s, pages, outg, inc,
    att, fxs, fxr, gps, gpr, gms, gmr, own, hss, hsr, order, slot_of, source,
    in_sem, a_send, a_recv, q_send, q_recv, kv_send, kv_recv, b_send,
    pg_send, pg_recv, ex_send, ex_recv, att_send, att_recv, o_send, o_recv, up_sem,
):
    s = lax.axis_index("seq")
    w = lax.axis_index("wide")
    n = lax.axis_index("narrow")
    x, yh = lax.div(w, 2), lax.rem(w, 2)
    yl, k = lax.div(n, 2), lax.rem(n, 2)
    y = 2 * yh + yl

    def at_y(step):
        other = lax.rem(y + step, 4)
        return (s, 2 * x + lax.div(other, 2), 2 * lax.rem(other, 2) + k)

    def unit_y(step, core):
        return 2 * lax.rem(y + step, 4) + core

    partner = (s, w, 2 * yl + 1 - k)
    across = (s, w, 2 * (1 - yl) + k)
    home = 2 * lax.rem(w, 4) + lax.div(w, 4)
    from_home = lax.div(w, 2) + 4 * lax.rem(w, 2)
    z_next = (lax.rem(s + 1, 16), w, n)
    z_prev = (lax.rem(s + 15, 16), w, n)
    x_next = (s, 2 * lax.rem(x + 1, 4) + yh, n)
    x_prev = (s, 2 * lax.rem(x + 3, 4) + yh, n)
    y_far = (s, 2 * x + 1 - yh, n)

    def send(src, dst, send_sem, recv_sem, device):
        copy = pltpu.make_async_remote_copy(
            src_ref=src, dst_ref=dst, send_sem=send_sem, recv_sem=recv_sem,
            device_id=device, device_id_type=MESH,
        )
        copy.start()
        pending.append(copy)
        return copy

    def arrived(dst, recv_sem):
        pltpu.make_async_remote_copy(
            src_ref=dst, dst_ref=dst, send_sem=b_send, recv_sem=recv_sem,
            device_id=partner, device_id_type=MESH,
        ).wait_recv()

    pending = []

    loads = []
    for number, (src, dst) in enumerate(
        ((tok_any, tok), (kvw_any, kvw), (qw_any, qw), (ow_any, ow))
    ):
        load = pltpu.make_async_copy(src, dst, in_sem.at[number])
        load.start()
        loads.append(load)

    barrier = pltpu.get_barrier_semaphore()
    near = (
        [(s, w, lax.rem(n + step, 4)) for step in (1, 2, 3)]
        + [z_next, z_prev, at_y(1), at_y(3), x_next, x_prev, y_far]
    )
    for device in near:
        pl.semaphore_signal(barrier, inc=1, device_id=device, device_id_type=MESH)

    @pl.when(home != w)
    def _():
        for other in (home, from_home):
            pl.semaphore_signal(
                barrier, inc=1, device_id=(s, other, n), device_id_type=MESH
            )

    loads[0].wait()
    loads[1].wait()
    for q in range(4):
        rows = pl.ds(q * QUARTER, QUARTER)
        local = tok[rows, :].astype(F32)
        norm = jnp.sum(local * local, axis=1, keepdims=True)
        part = (local * gain[...]).astype(BF16)
        scaled[rows, :] = part
        kvp[q, 0:QUARTER, :] = jnp.dot(part, kvw[...], preferred_element_type=F32)
        turned = jnp.transpose(jnp.broadcast_to(norm, (QUARTER, QUARTER)))
        kvp[q, QUARTER:QUARTER + 8, :] = turned[0:8, :]

    pl.semaphore_wait(barrier, len(near) + 2 * lax.div(lax.rem(w, 7) + 6, 7))

    for step in (2, 3, 1):
        q = lax.rem(n + step, 4)
        send(kvp.at[q], kvr.at[n], a_send.at[step - 1], a_recv.at[n], (s, w, q))
    pl.semaphore_signal(up_sem, inc=1, device_id=z_prev, device_id_type=MESH)

    loads[2].wait()
    for j in range(2):
        q = 2 * j + 1 - k
        rows = pl.ds(pl.multiple_of(q * QUARTER, QUARTER), QUARTER)
        qs1[j] = jnp.dot(scaled[rows, :], qw[...], preferred_element_type=F32).astype(BF16)
    q1 = send(qs1, qr1, q_send.at[0], q_recv.at[0], partner)

    index = (
        s * BLOCK + n * QUARTER
        + lax.broadcasted_iota(jnp.int32, (QUARTER, HD), 0)
    )
    end0 = lens[0]
    end1 = end0 + lens[1]
    end2 = end1 + lens[2]
    begin = jnp.where(index >= end0, end0, 0)
    begin = jnp.where(index >= end1, end1, begin)
    begin = jnp.where(index >= end2, end2, begin)
    angle = (index - begin).astype(F32) * freq[...]
    lane = lax.broadcasted_iota(jnp.int32, (QUARTER, HD), 1)
    cos_s[...] = jnp.cos(angle)
    sine = jnp.sin(angle)
    sin_s[...] = jnp.where(lane < HD // 2, -sine, sine)

    for step in (1, 2, 3):
        q = lax.rem(n + step, 4)
        arrived(kvr.at[q], a_recv.at[q])
    total = kvp[n] + kvr[lax.rem(n + 1, 4)] + kvr[lax.rem(n + 2, 4)] + kvr[lax.rem(n + 3, 4)]
    rinv = lax.rsqrt(total[QUARTER:QUARTER + 1, :] / WIDTH + EPS)
    rinv = jnp.transpose(jnp.broadcast_to(rinv, (QUARTER, QUARTER)))
    rinv_s[...] = rinv

    def rotate(values):
        return values * cos_s[...] + pltpu.roll(values, HD // 2, 1) * sin_s[...]

    plain = total[0:QUARTER, :] * rinv
    final = jnp.where(w < KV_HEADS, rotate(plain), plain).astype(BF16)
    mykv[...] = final
    pages[pl.ds(4 * n, 4)] = final.reshape(4, 32, HD)

    unit = unit_y(0, k)
    target = 4 * lax.div(w, 4) + n
    move = pltpu.make_async_remote_copy(
        src_ref=mykv, dst_ref=kv_all.at[0, target], send_sem=b_send,
        recv_sem=kv_recv.at[0, target], device_id=(s, home, n), device_id_type=MESH,
    )
    stay = pltpu.make_async_copy(mykv, kv_all.at[0, unit], kv_recv.at[0, unit])

    @pl.when(home != w)
    def _():
        move.start()

    @pl.when(home == w)
    def _():
        stay.start()

    for j in range(2):
        q = 2 * j + k
        rows = pl.ds(pl.multiple_of(q * QUARTER, QUARTER), QUARTER)
        qf[j] = jnp.dot(scaled[rows, :], qw[...], preferred_element_type=F32)
    arrived(qr1, q_recv.at[0])
    qs2[...] = (qf[1 - yl] + qr1[1 - yl].astype(F32)).astype(BF16)
    send(qs2, qr2, q_send.at[1], q_recv.at[1], across)

    @pl.when(home != w)
    def _():
        move.wait_send()
        pltpu.make_async_remote_copy(
            src_ref=mykv, dst_ref=kv_all.at[0, unit], send_sem=b_send,
            recv_sem=kv_recv.at[0, unit], device_id=(s, home, n), device_id_type=MESH,
        ).wait_recv()

    @pl.when(home == w)
    def _():
        stay.wait()

    def spread(block, piece, device, action):
        send(
            kv_all.at[block, piece], kv_all.at[block, piece],
            kv_send.at[block, action], kv_recv.at[block, piece], device,
        )

    def landed(block, piece):
        arrived(kv_all.at[block, piece], kv_recv.at[block, piece])

    def own_unit(block):
        if block > 0:
            landed(block, unit)
        if block < BACK:
            send(
                kv_all.at[block, unit], kv_all.at[block + 1, unit],
                kv_send.at[block, 0], kv_recv.at[block + 1, unit], z_next,
            )
        spread(block, unit, at_y(1), 1)
        spread(block, unit, at_y(3), 2)
        spread(block, unit, partner, 3)

    def near_units(block):
        landed(block, unit_y(1, k))
        landed(block, unit_y(3, k))
        spread(block, unit_y(3 + 2 * k, k), at_y(1 + 2 * k), 4)
        spread(block, unit_y(1, k), partner, 5)
        spread(block, unit_y(3, k), partner, 6)

    def far_unit(block):
        landed(block, unit_y(2, k))
        spread(block, unit_y(2, k), partner, 7)

    scale = 1.0 / (HD ** 0.5 * float(np.log(2.0)))

    def attend(block):
        for step in range(4):
            landed(block, unit_y(step, 1 - k))
        keys = kv_all[block, 0:4].reshape(BLOCK, HD)
        values = kv_all[block, 4:8].reshape(BLOCK, HD)
        key_index = (s - block) * BLOCK + lax.broadcasted_iota(jnp.int32, (QUARTER, BLOCK), 1)
        row = s * BLOCK + n * QUARTER + lax.broadcasted_iota(jnp.int32, (QUARTER, 1), 0)
        first = jnp.where(row >= end0, end0, 0)
        first = jnp.where(row >= end1, end1, first)
        first = jnp.where(row >= end2, end2, first)
        allowed = key_index >= first
        if block == 0:
            allowed = allowed & (key_index <= row)

        def head(h, carry):
            scores = lax.dot_general(
                queries[h], keys, (((1,), (1,)), ((), ())), preferred_element_type=F32
            )
            masked = jnp.where(allowed, scores, NEG)
            top = jnp.max(masked, axis=1, keepdims=True)
            if block > 0:
                old = m_s[h]
                new = jnp.maximum(old, top)
                alpha = jnp.exp2((old - new) * scale)
                weights = jnp.exp2((masked - new[:, 0:1]) * scale)
                l_s[h] = l_s[h] * alpha + jnp.sum(weights, axis=1, keepdims=True)
                acc_s[h] = acc_s[h] * alpha + jnp.dot(
                    weights.astype(BF16), values, preferred_element_type=F32
                )
                m_s[h] = new
            else:
                weights = jnp.exp2((masked - top) * scale)
                m_s[h] = jnp.broadcast_to(top, (QUARTER, HD))
                l_s[h] = jnp.broadcast_to(
                    jnp.sum(weights, axis=1, keepdims=True), (QUARTER, HD)
                )
                acc_s[h] = jnp.dot(weights.astype(BF16), values, preferred_element_type=F32)
            return carry

        lax.fori_loop(0, 4, head, 0)

    def finish_queries():
        arrived(qr2, q_recv.at[1])
        summed = qf[yl] + qr1[yl].astype(F32) + qr2[...].astype(F32)
        for h in range(4):
            value = summed[:, h * HD:(h + 1) * HD] * rinv_s[...]
            queries[h] = rotate(value).astype(BF16)

    def gather_pages():
        for step in (1, 2, 3):
            send(
                pages.at[pl.ds(4 * n, 4)], pages.at[pl.ds(4 * n, 4)],
                pg_send.at[step - 1], pg_recv.at[n], (s, w, lax.rem(n + step, 4)),
            )

    def page_order():
        def owned(r, carry):
            found = jnp.int32(0)
            for j in range(16):
                owner = lax.shift_right_logical(table[16 * s + j], 4)
                found = jnp.where(owner == r, j, found)
            order[r] = found
            place = jnp.int32(0)
            for j in range(16):
                slot = table[16 * r + j]
                mine = lax.shift_right_logical(slot, 4) == s
                place = jnp.where(mine, slot & 15, place)
            slot_of[r] = place
            return carry

        lax.fori_loop(0, 16, owned, 0)

        def placed(slot, carry):
            found = jnp.int32(0)
            for j in range(16):
                found = jnp.where(slot_of[j] == slot, j, found)
            source[slot] = found
            return carry

        lax.fori_loop(0, 16, placed, 0)

    def pack_pages():
        for step in (1, 2, 3):
            q = lax.rem(n + step, 4)
            arrived(pages.at[pl.ds(4 * q, 4)], pg_recv.at[q])
        for r in range(16):
            outg[r] = pages[order[r]]
        inc[s] = outg[s]

    def send_pages():
        for step in (8, 7, 9, 6, 10, 5, 11, 4, 12, 3, 13, 2, 14, 1, 15):
            r = lax.rem(s + step, 16)
            send(outg.at[r], inc.at[s], ex_send.at[step - 1], ex_recv.at[s], (r, w, n))

    for t in range(BACK + 4):
        if t <= BACK:
            own_unit(t)
        if 1 <= t <= 7:
            pl.semaphore_wait(up_sem, 1)
            if t < 7:
                pl.semaphore_signal(up_sem, inc=1, device_id=z_prev, device_id_type=MESH)
        if t == 1:
            finish_queries()
            gather_pages()
        if t == 2:
            page_order()
        if 0 <= t - 1 <= BACK:
            near_units(t - 1)
        if 0 <= t - 2 <= BACK:
            far_unit(t - 2)
        if t == 7:
            pack_pages()
        if 0 <= t - 3 <= BACK:
            attend(t - 3)

    for h in range(4):
        att[n, :, h * HD:(h + 1) * HD] = (acc_s[h] / l_s[h]).astype(BF16)
    send(att.at[n], att.at[n], att_send.at[0], att_recv.at[n], across)
    send(att.at[n], att.at[n], att_send.at[1], att_recv.at[n], partner)
    send_pages()
    loads[3].wait()
    other = 2 * (1 - yl) + k
    arrived(att.at[other], att_recv.at[other])
    send(att.at[other], att.at[other], att_send.at[2], att_recv.at[other], partner)
    for q in (2 * yl + 1 - k, 2 * (1 - yl) + 1 - k):
        arrived(att.at[q], att_recv.at[q])

    def product(step):
        return jnp.dot(att[lax.rem(x + step, 4)], ow[...], preferred_element_type=F32)

    half = WIDTH // 8
    far = product(2)
    fxs[0] = far[:, 0:half].astype(BF16)
    fxs[1] = far[:, half:].astype(BF16)
    send(fxs.at[0], fxr.at[0], o_send.at[0], o_recv.at[0], x_next)
    send(fxs.at[1], fxr.at[1], o_send.at[1], o_recv.at[1], x_prev)
    up = product(1)
    down = product(3)
    gps[1] = up[:, half:].astype(BF16)
    gms[0] = down[:, 0:half].astype(BF16)
    send(gps.at[1], gpr.at[1], o_send.at[2], o_recv.at[2], x_next)
    send(gms.at[0], gmr.at[0], o_send.at[3], o_recv.at[3], x_prev)
    own[...] = product(0)
    arrived(fxr.at[0], o_recv.at[0])
    gps[0] = (up[:, 0:half] + fxr[0].astype(F32)).astype(BF16)
    send(gps.at[0], gpr.at[0], o_send.at[4], o_recv.at[4], x_next)
    arrived(fxr.at[1], o_recv.at[1])
    gms[1] = (down[:, half:] + fxr[1].astype(F32)).astype(BF16)
    send(gms.at[1], gmr.at[1], o_send.at[5], o_recv.at[5], x_prev)

    for step in range(1, 16):
        r = lax.rem(s + step, 16)
        arrived(inc.at[r], ex_recv.at[r])
    for slot in range(16):
        cache[slot] = inc[source[slot]]

    for sem, ref in ((2, gpr.at[1]), (3, gmr.at[0]), (4, gpr.at[0]), (5, gmr.at[1])):
        arrived(ref, o_recv.at[sem])
    away = pl.ds(pl.multiple_of(64 * (1 - yh), 64), 64)
    mine = pl.ds(pl.multiple_of(64 * yh, 64), 64)

    def summed(rows, part):
        cols = pl.ds(part * half, half)
        return own[rows, cols] + gpr[part, rows, :].astype(F32) + gmr[part, rows, :].astype(F32)

    for part in range(2):
        hss[part] = summed(away, part).astype(BF16)
        send(hss.at[part], hsr.at[part], o_send.at[6 + part], o_recv.at[6 + part], y_far)
    rows = pl.ds(pl.multiple_of(64 * w, 64), 64)
    for part in range(2):
        cols = pl.ds(part * half, half)
        base = tok[rows, cols].astype(F32) + summed(mine, part)
        arrived(hsr.at[part], o_recv.at[6 + part])
        hid[:, cols] = (base + hsr[part].astype(F32)).astype(BF16)

    for copy in pending:
        copy.wait_send()


def on_device(tokens, norm_gain, q_weight, kv_weight, out_weight, lengths, page_table, freq):
    vmem = pl.BlockSpec(memory_space=pltpu.VMEM)
    smem = pl.BlockSpec(memory_space=pltpu.SMEM)
    hbm = pl.BlockSpec(memory_space=pl.ANY)
    dma = pltpu.SemaphoreType.DMA
    part = WIDTH // 4
    half = part // 2
    return pl.pallas_call(
        kernel,
        out_shape=(
            jax.ShapeDtypeStruct((64, part), BF16),
            jax.ShapeDtypeStruct((16, 32, HD), BF16),
        ),
        in_specs=[smem, smem, vmem, vmem, hbm, hbm, hbm, hbm],
        out_specs=(vmem, vmem),
        scratch_shapes=[
            pltpu.VMEM((BLOCK, part), BF16),
            pltpu.VMEM((part, HD), BF16),
            pltpu.VMEM((part, BLOCK), BF16),
            pltpu.VMEM((BLOCK, part), BF16),
            pltpu.VMEM((BLOCK, part), BF16),
            pltpu.VMEM((4, QUARTER + 8, HD), F32),
            pltpu.VMEM((4, QUARTER + 8, HD), F32),
            pltpu.VMEM((2, QUARTER, BLOCK), F32),
            pltpu.VMEM((2, QUARTER, BLOCK), BF16),
            pltpu.VMEM((2, QUARTER, BLOCK), BF16),
            pltpu.VMEM((QUARTER, BLOCK), BF16),
            pltpu.VMEM((QUARTER, BLOCK), BF16),
            pltpu.VMEM((QUARTER, HD), BF16),
            pltpu.VMEM((BACK + 1, 8, QUARTER, HD), BF16),
            pltpu.VMEM((4, QUARTER, HD), BF16),
            pltpu.VMEM((4, QUARTER, HD), F32),
            pltpu.VMEM((4, QUARTER, HD), F32),
            pltpu.VMEM((4, QUARTER, HD), F32),
            pltpu.VMEM((QUARTER, HD), F32),
            pltpu.VMEM((QUARTER, HD), F32),
            pltpu.VMEM((QUARTER, HD), F32),
            pltpu.VMEM((16, 32, HD), BF16),
            pltpu.VMEM((16, 32, HD), BF16),
            pltpu.VMEM((16, 32, HD), BF16),
            pltpu.VMEM((4, QUARTER, BLOCK), BF16),
            pltpu.VMEM((2, QUARTER, half), BF16),
            pltpu.VMEM((2, QUARTER, half), BF16),
            pltpu.VMEM((2, QUARTER, half), BF16),
            pltpu.VMEM((2, QUARTER, half), BF16),
            pltpu.VMEM((2, QUARTER, half), BF16),
            pltpu.VMEM((2, QUARTER, half), BF16),
            pltpu.VMEM((QUARTER, part), F32),
            pltpu.VMEM((2, 64, half), BF16),
            pltpu.VMEM((2, 64, half), BF16),
            pltpu.SMEM((16,), jnp.int32),
            pltpu.SMEM((16,), jnp.int32),
            pltpu.SMEM((16,), jnp.int32),
            dma((4,)),
            dma((3,)),
            dma((4,)),
            dma((2,)),
            dma((2,)),
            dma((BACK + 1, 8)),
            dma((BACK + 1, 8)),
            dma,
            dma((3,)),
            dma((4,)),
            dma((15,)),
            dma((16,)),
            dma((3,)),
            dma((4,)),
            dma((8,)),
            dma((8,)),
            pltpu.SemaphoreType.REGULAR,
        ],
        compiler_params=pltpu.CompilerParams(collective_id=0, has_side_effects=True),
    )(lengths, page_table, norm_gain[None, :], freq, tokens, kv_weight, q_weight, out_weight)


def solution(mesh):
    half = HD // 2
    power = THETA ** (-np.arange(half, dtype=np.float64) * 2.0 / HD)
    freq = np.concatenate([power, power]).astype(np.float32)[None, :]
    placed = (
        P("seq", "narrow"),
        P("narrow"),
        P("narrow", "wide"),
        P("narrow", "wide"),
        P("wide", "narrow"),
        P(),
        P(),
    )

    def local(*args):
        return on_device(*args, jnp.asarray(freq))

    return jax.shard_map(
        local,
        mesh=mesh,
        in_specs=placed,
        out_specs=(P(("seq", "wide"), "narrow"), P("seq", None, "wide")),
        check_vma=False,
    )
```

```python
import jax
import jax.numpy as jnp
import numpy as np
from jax import lax
from jax.experimental import pallas as pl
from jax.experimental.pallas import tpu as pltpu
from jax.sharding import PartitionSpec as P

HEADS = 32
KV_HEADS = 4
HD = 128
WIDTH = 4096
BLOCK = 512
QUARTER = 128
EPS = 1e-05
THETA = 5000000.0
NEG = -1e30
BACK = 8
MESH = pl.DeviceIdType.MESH
F32 = jnp.float32
BF16 = jnp.bfloat16


def kernel(
    lens, table, gain, freq, tok_any, kvw_any, qw_any, ow_any,
    hid, cache,
    tok, kvw, qw, ow, scaled, kvp, kvr, qf, qs1, qr1, qs2, qr2, mykv,
    kv_all, queries, m_s, l_s, acc_s, cos_s, sin_s, rinv_s, pages, outg, inc,
    att, fxs, fxr, gps, gpr, gms, gmr, up, down, own, hss, hsr, order, slot_of, source,
    in_sem, a_send, a_recv, q_send, q_recv, kv_send, kv_recv, z_send, b_send,
    pg_send, pg_recv, ex_send, ex_recv, att_send, att_recv, o_send, o_recv, up_sem, down_sem,
):
    s = lax.axis_index("seq")
    w = lax.axis_index("wide")
    n = lax.axis_index("narrow")
    x, yh = lax.div(w, 2), lax.rem(w, 2)
    yl, k = lax.div(n, 2), lax.rem(n, 2)
    y = 2 * yh + yl

    def at_y(step):
        other = lax.rem(y + step, 4)
        return (s, 2 * x + lax.div(other, 2), 2 * lax.rem(other, 2) + k)

    def unit_y(step, core):
        return 2 * lax.rem(y + step, 4) + core

    partner = (s, w, 2 * yl + 1 - k)
    across = (s, w, 2 * (1 - yl) + k)
    home = 2 * lax.rem(w, 4) + lax.div(w, 4)
    from_home = lax.div(w, 2) + 4 * lax.rem(w, 2)
    z_next = (lax.rem(s + 1, 16), w, n)
    z_prev = (lax.rem(s + 15, 16), w, n)
    z_jump = (lax.rem(s + 3, 16), w, n)
    z_back = (lax.rem(s + 13, 16), w, n)
    x_next = (s, 2 * lax.rem(x + 1, 4) + yh, n)
    x_prev = (s, 2 * lax.rem(x + 3, 4) + yh, n)
    y_far = (s, 2 * x + 1 - yh, n)

    def send(src, dst, send_sem, recv_sem, device):
        copy = pltpu.make_async_remote_copy(
            src_ref=src, dst_ref=dst, send_sem=send_sem, recv_sem=recv_sem,
            device_id=device, device_id_type=MESH,
        )
        copy.start()
        pending.append(copy)

    def arrived(dst, recv_sem):
        pltpu.make_async_remote_copy(
            src_ref=dst, dst_ref=dst, send_sem=b_send, recv_sem=recv_sem,
            device_id=partner, device_id_type=MESH,
        ).wait_recv()

    pending = []

    loads = []
    for number, (src, dst) in enumerate(
        ((tok_any, tok), (kvw_any, kvw), (qw_any, qw), (ow_any, ow))
    ):
        load = pltpu.make_async_copy(src, dst, in_sem.at[number])
        load.start()
        loads.append(load)

    barrier = pltpu.get_barrier_semaphore()
    near = (
        [(s, w, lax.rem(n + step, 4)) for step in (1, 2, 3)]
        + [z_next, z_prev, z_jump, z_back, at_y(1), at_y(3), x_next, x_prev, y_far]
    )
    for device in near:
        pl.semaphore_signal(barrier, inc=1, device_id=device, device_id_type=MESH)

    @pl.when(home != w)
    def _():
        for other in (home, from_home):
            pl.semaphore_signal(
                barrier, inc=1, device_id=(s, other, n), device_id_type=MESH
            )

    loads[0].wait()
    loads[1].wait()
    for q in range(4):
        rows = pl.ds(q * QUARTER, QUARTER)
        local = tok[rows, :].astype(F32)
        norm = jnp.sum(local * local, axis=1, keepdims=True)
        part = (local * gain[...]).astype(BF16)
        scaled[rows, :] = part
        kvp[q, 0:QUARTER, :] = jnp.dot(part, kvw[...], preferred_element_type=F32)
        turned = jnp.transpose(jnp.broadcast_to(norm, (QUARTER, QUARTER)))
        kvp[q, QUARTER:QUARTER + 8, :] = turned[0:8, :]

    pl.semaphore_wait(barrier, len(near) + 2 * lax.div(lax.rem(w, 7) + 6, 7))

    for step in (2, 3, 1):
        q = lax.rem(n + step, 4)
        send(kvp.at[q], kvr.at[n], a_send.at[step - 1], a_recv.at[n], (s, w, q))

    def pass_on(first):
        if first != 1:
            pl.semaphore_wait(up_sem, 1)
            pl.semaphore_wait(down_sem, 1)
        if first < 2:
            pl.semaphore_signal(up_sem, inc=1, device_id=z_prev, device_id_type=MESH)
            pl.semaphore_signal(down_sem, inc=1, device_id=z_next, device_id_type=MESH)

    pass_on(1)

    loads[2].wait()
    for j in range(2):
        q = 2 * j + 1 - k
        rows = pl.ds(pl.multiple_of(q * QUARTER, QUARTER), QUARTER)
        qs1[j] = jnp.dot(scaled[rows, :], qw[...], preferred_element_type=F32).astype(BF16)
    send(qs1, qr1, q_send.at[0], q_recv.at[0], partner)

    index = (
        s * BLOCK + n * QUARTER
        + lax.broadcasted_iota(jnp.int32, (QUARTER, HD), 0)
    )
    end0 = lens[0]
    end1 = end0 + lens[1]
    end2 = end1 + lens[2]
    begin = jnp.where(index >= end0, end0, 0)
    begin = jnp.where(index >= end1, end1, begin)
    begin = jnp.where(index >= end2, end2, begin)
    angle = (index - begin).astype(F32) * freq[...]
    lane = lax.broadcasted_iota(jnp.int32, (QUARTER, HD), 1)
    cos_s[...] = jnp.cos(angle)
    sine = jnp.sin(angle)
    sin_s[...] = jnp.where(lane < HD // 2, -sine, sine)

    for step in (1, 2, 3):
        q = lax.rem(n + step, 4)
        arrived(kvr.at[q], a_recv.at[q])
    total = kvp[n] + kvr[lax.rem(n + 1, 4)] + kvr[lax.rem(n + 2, 4)] + kvr[lax.rem(n + 3, 4)]
    rinv = lax.rsqrt(total[QUARTER:QUARTER + 1, :] / WIDTH + EPS)
    rinv = jnp.transpose(jnp.broadcast_to(rinv, (QUARTER, QUARTER)))
    rinv_s[...] = rinv

    def rotate(values):
        return values * cos_s[...] + pltpu.roll(values, HD // 2, 1) * sin_s[...]

    plain = total[0:QUARTER, :] * rinv
    final = jnp.where(w < KV_HEADS, rotate(plain), plain).astype(BF16)
    mykv[...] = final
    pages[pl.ds(4 * n, 4)] = final.reshape(4, 32, HD)

    unit = unit_y(0, k)
    target = 4 * lax.div(w, 4) + n
    move = pltpu.make_async_remote_copy(
        src_ref=mykv, dst_ref=kv_all.at[0, target], send_sem=b_send,
        recv_sem=kv_recv.at[0, target], device_id=(s, home, n), device_id_type=MESH,
    )
    stay = pltpu.make_async_copy(mykv, kv_all.at[0, unit], kv_recv.at[0, unit])

    @pl.when(home != w)
    def _():
        move.start()

    @pl.when(home == w)
    def _():
        stay.start()

    for j in range(2):
        q = 2 * j + k
        rows = pl.ds(pl.multiple_of(q * QUARTER, QUARTER), QUARTER)
        qf[j] = jnp.dot(scaled[rows, :], qw[...], preferred_element_type=F32)
    arrived(qr1, q_recv.at[0])
    qs2[...] = (qf[1 - yl] + qr1[1 - yl].astype(F32)).astype(BF16)
    send(qs2, qr2, q_send.at[1], q_recv.at[1], across)

    @pl.when(home != w)
    def _():
        move.wait_send()
        pltpu.make_async_remote_copy(
            src_ref=mykv, dst_ref=kv_all.at[0, unit], send_sem=b_send,
            recv_sem=kv_recv.at[0, unit], device_id=(s, home, n), device_id_type=MESH,
        ).wait_recv()

    @pl.when(home == w)
    def _():
        stay.wait()

    hops = {0: (1, 3), 1: (1,), 3: (1, 3), 4: (1,), 6: (1,), 7: (1,)}

    def piece_copy(block, action):
        step, target = ((0, at_y(1)), (0, at_y(3)), (0, partner), (None, at_y(1 + 2 * k)),
                        (1, partner), (3, partner), (2, partner))[action]
        piece = unit_y(3 + 2 * k if step is None else step, k)
        return pltpu.make_async_remote_copy(
            src_ref=kv_all.at[block, piece], dst_ref=kv_all.at[block, piece],
            send_sem=kv_send.at[block, action], recv_sem=kv_recv.at[block, piece],
            device_id=target, device_id_type=MESH,
        )

    def jump_copy(block, step):
        return pltpu.make_async_remote_copy(
            src_ref=kv_all.at[block, unit], dst_ref=kv_all.at[block + step, unit],
            send_sem=z_send.at[block, step // 2], recv_sem=kv_recv.at[block + step, unit],
            device_id=(lax.rem(s + step, 16), w, n), device_id_type=MESH,
        )

    def spread(block, *actions):
        for action in actions:
            piece_copy(block, action).start()

    def landed(block, piece):
        arrived(kv_all.at[block, piece], kv_recv.at[block, piece])

    def own_unit(block):
        if block > 0:
            landed(block, unit)
        for step in hops.get(block, ()):
            pl.when(s < 16 - step)(lambda step=step: jump_copy(block, step).start())
        spread(block, 0, 1, 2)

    def near_units(block):
        landed(block, unit_y(1, k))
        landed(block, unit_y(3, k))
        spread(block, 3, 4, 5)

    def far_unit(block):
        landed(block, unit_y(2, k))
        spread(block, 6)

    def settle(block):
        for step in hops.get(block, ()):
            pl.when(s < 16 - step)(lambda step=step: jump_copy(block, step).wait_send())
        for action in range(7):
            piece_copy(block, action).wait_send()

    def present(block, action):
        if block == 0:
            action(0)
        else:
            pl.when(s >= block)(lambda: action(block))

    scale = 1.0 / (HD ** 0.5 * float(np.log(2.0)))

    def attend(block):
        for step in range(4):
            landed(block, unit_y(step, 1 - k))
        keys = kv_all[block, 0:4].reshape(BLOCK, HD)
        values = kv_all[block, 4:8].reshape(BLOCK, HD)
        shape = (4, QUARTER, BLOCK)
        key_index = (s - block) * BLOCK + lax.broadcasted_iota(jnp.int32, shape, 2)
        row = s * BLOCK + n * QUARTER + lax.broadcasted_iota(jnp.int32, (4, QUARTER, 1), 1)
        first = jnp.where(row >= end0, end0, 0)
        first = jnp.where(row >= end1, end1, first)
        first = jnp.where(row >= end2, end2, first)
        allowed = key_index >= first
        if block == 0:
            allowed = allowed & (key_index <= row)
        scores = lax.dot_general(
            queries[...], keys, (((1,), (1,)), ((), ())), preferred_element_type=F32
        )
        masked = jnp.where(allowed.reshape(BLOCK, BLOCK), scores, NEG)
        top = jnp.broadcast_to(jnp.max(masked, axis=1, keepdims=True), (BLOCK, HD))
        if block > 0:
            old = m_s[...]
            top = jnp.maximum(old, top)
        weights = jnp.exp2((masked - jnp.concatenate([top] * 4, axis=1)) * scale)
        lanes = (weights[:, 0:HD] + weights[:, HD:2 * HD]) + (
            weights[:, 2 * HD:3 * HD] + weights[:, 3 * HD:]
        )
        mixed = jnp.dot(weights.astype(BF16), values, preferred_element_type=F32)
        if block > 0:
            alpha = jnp.exp2((old - top) * scale)
            lanes = l_s[...] * alpha + lanes
            mixed = acc_s[...] * alpha + mixed
        m_s[...] = top
        l_s[...] = lanes
        acc_s[...] = mixed

    def finish_queries():
        arrived(qr2, q_recv.at[1])
        summed = qf[yl] + qr1[yl].astype(F32) + qr2[...].astype(F32)
        for h in range(4):
            value = summed[:, h * HD:(h + 1) * HD] * rinv_s[...]
            queries[h * QUARTER:(h + 1) * QUARTER, :] = rotate(value).astype(BF16)

    def gather_pages():
        for step in (1, 2, 3):
            send(
                pages.at[pl.ds(4 * n, 4)], pages.at[pl.ds(4 * n, 4)],
                pg_send.at[step - 1], pg_recv.at[n], (s, w, lax.rem(n + step, 4)),
            )

    def page_order():
        def owned(r, carry):
            found = jnp.int32(0)
            for j in range(16):
                owner = lax.shift_right_logical(table[16 * s + j], 4)
                found = jnp.where(owner == r, j, found)
            order[r] = found
            place = jnp.int32(0)
            for j in range(16):
                slot = table[16 * r + j]
                mine = lax.shift_right_logical(slot, 4) == s
                place = jnp.where(mine, slot & 15, place)
            slot_of[r] = place
            return carry

        lax.fori_loop(0, 16, owned, 0)

        def placed(slot, carry):
            found = jnp.int32(0)
            for j in range(16):
                found = jnp.where(slot_of[j] == slot, j, found)
            source[slot] = found
            return carry

        lax.fori_loop(0, 16, placed, 0)

    def pack_pages():
        for step in (1, 2, 3):
            q = lax.rem(n + step, 4)
            arrived(pages.at[pl.ds(4 * q, 4)], pg_recv.at[q])
        for r in range(16):
            outg[r] = pages[order[r]]
        inc[s] = outg[s]

    def send_pages():
        for step in (8, 7, 9, 6, 10, 5, 11, 4, 12, 3, 13, 2, 14, 1, 15):
            r = lax.rem(s + step, 16)
            send(outg.at[r], inc.at[s], ex_send.at[step - 1], ex_recv.at[s], (r, w, n))

    reach = {0: 0.0, 1: 2.4, 2: 4.8, 3: 3.9, 4: 6.3, 5: 8.7, 6: 7.8, 7: 10.2, 8: 12.6}
    events = [(2.5, 0, finish_queries, None), (3.0, 0, gather_pages, None),
              (5.0, 0, page_order, None), (9.5, 0, pack_pages, None), (14.0, 0, send_pages, None)]
    for level in range(8):
        events.append((2.0 + 1.5 * level, 1, pass_on, 0 if level < 7 else 2))
    for block, time in reach.items():
        events.append((time, 2, own_unit, block))
        events.append((time + 2.6, 3, near_units, block))
        events.append((time + 5.2, 4, far_unit, block))
        events.append((time + 6.8, 5, attend, block))
    for _, kind, action, value in sorted(events, key=lambda e: e[:2]):
        if kind == 0:
            action()
        elif kind == 1:
            action(value)
        else:
            present(value, action)

    mixed = acc_s[...] / jnp.sum(l_s[...], axis=1, keepdims=True)
    for h in range(4):
        att[n, :, h * HD:(h + 1) * HD] = mixed[h * QUARTER:(h + 1) * QUARTER].astype(BF16)
    send(att.at[n], att.at[n], att_send.at[0], att_recv.at[n], across)
    send(att.at[n], att.at[n], att_send.at[1], att_recv.at[n], partner)
    loads[3].wait()
    other = 2 * (1 - yl) + k
    arrived(att.at[other], att_recv.at[other])
    send(att.at[other], att.at[other], att_send.at[2], att_recv.at[other], partner)
    for q in (2 * yl + 1 - k, 2 * (1 - yl) + 1 - k):
        arrived(att.at[q], att_recv.at[q])

    def product(step):
        return jnp.dot(att[lax.rem(x + step, 4)], ow[...], preferred_element_type=F32)

    half = WIDTH // 8
    left, right = pl.ds(0, half), pl.ds(half, half)
    away = pl.ds(pl.multiple_of(64 * (1 - yh), 64), 64)
    mine = pl.ds(pl.multiple_of(64 * yh, 64), 64)

    def give(src, dst, part, rows, number, device):
        send(
            src.at[part, rows, :], dst.at[part, rows, :],
            o_send.at[number], o_recv.at[number], device,
        )

    def got(dst, part, rows, number):
        arrived(dst.at[part, rows, :], o_recv.at[number])

    far = product(2)
    fxs[0] = far[:, 0:half].astype(BF16)
    fxs[1] = far[:, half:].astype(BF16)
    give(fxs, fxr, 0, away, 0, x_next)
    give(fxs, fxr, 1, away, 1, x_prev)
    up[...] = product(1)
    gps[1] = up[:, right].astype(BF16)
    give(gps, gpr, 1, away, 2, x_next)
    down[...] = product(3)
    gms[0] = down[:, left].astype(BF16)
    give(gms, gmr, 0, away, 3, x_prev)
    give(fxs, fxr, 0, mine, 4, x_next)
    give(fxs, fxr, 1, mine, 5, x_prev)
    own[...] = product(0)
    for rows, number, direct in ((away, 0, None), (mine, 4, mine)):
        if direct is not None:
            give(gps, gpr, 1, mine, 6, x_next)
            give(gms, gmr, 0, mine, 7, x_prev)
        got(fxr, 0, rows, number)
        gps[0, rows, :] = (up[rows, left] + fxr[0, rows, :].astype(F32)).astype(BF16)
        give(gps, gpr, 0, rows, 8 + number, x_next)
        got(fxr, 1, rows, number + 1)
        gms[1, rows, :] = (down[rows, right] + fxr[1, rows, :].astype(F32)).astype(BF16)
        give(gms, gmr, 1, rows, 9 + number, x_prev)

    for step in range(1, 16):
        r = lax.rem(s + step, 16)
        arrived(inc.at[r], ex_recv.at[r])
    for slot in range(16):
        cache[slot] = inc[source[slot]]

    def summed(rows, part):
        cols = pl.ds(part * half, half)
        return own[rows, cols] + gpr[part, rows, :].astype(F32) + gmr[part, rows, :].astype(F32)

    got(gpr, 1, away, 2)
    got(gmr, 1, away, 9)
    hss[1] = summed(away, 1).astype(BF16)
    send(hss.at[1], hsr.at[1], o_send.at[15], o_recv.at[15], y_far)
    got(gmr, 0, away, 3)
    got(gpr, 0, away, 8)
    hss[0] = summed(away, 0).astype(BF16)
    send(hss.at[0], hsr.at[0], o_send.at[14], o_recv.at[14], y_far)
    got(gpr, 1, mine, 6)
    got(gmr, 0, mine, 7)
    got(gpr, 0, mine, 12)
    got(gmr, 1, mine, 13)
    rows = pl.ds(pl.multiple_of(64 * w, 64), 64)
    for part in (1, 0):
        cols = pl.ds(part * half, half)
        base = tok[rows, cols].astype(F32) + summed(mine, part)
        arrived(hsr.at[part], o_recv.at[14 + part])
        hid[:, cols] = (base + hsr[part].astype(F32)).astype(BF16)

    for copy in pending:
        copy.wait_send()
    for block in range(BACK + 1):
        present(block, settle)


def on_device(tokens, norm_gain, q_weight, kv_weight, out_weight, lengths, page_table, freq):
    vmem = pl.BlockSpec(memory_space=pltpu.VMEM)
    smem = pl.BlockSpec(memory_space=pltpu.SMEM)
    hbm = pl.BlockSpec(memory_space=pl.ANY)
    dma = pltpu.SemaphoreType.DMA
    part = WIDTH // 4
    half = part // 2
    return pl.pallas_call(
        kernel,
        out_shape=(
            jax.ShapeDtypeStruct((64, part), BF16),
            jax.ShapeDtypeStruct((16, 32, HD), BF16),
        ),
        in_specs=[smem, smem, vmem, vmem, hbm, hbm, hbm, hbm],
        out_specs=(vmem, vmem),
        scratch_shapes=[
            pltpu.VMEM((BLOCK, part), BF16),
            pltpu.VMEM((part, HD), BF16),
            pltpu.VMEM((part, BLOCK), BF16),
            pltpu.VMEM((BLOCK, part), BF16),
            pltpu.VMEM((BLOCK, part), BF16),
            pltpu.VMEM((4, QUARTER + 8, HD), F32),
            pltpu.VMEM((4, QUARTER + 8, HD), F32),
            pltpu.VMEM((2, QUARTER, BLOCK), F32),
            pltpu.VMEM((2, QUARTER, BLOCK), BF16),
            pltpu.VMEM((2, QUARTER, BLOCK), BF16),
            pltpu.VMEM((QUARTER, BLOCK), BF16),
            pltpu.VMEM((QUARTER, BLOCK), BF16),
            pltpu.VMEM((QUARTER, HD), BF16),
            pltpu.VMEM((BACK + 1, 8, QUARTER, HD), BF16),
            pltpu.VMEM((BLOCK, HD), BF16),
            pltpu.VMEM((BLOCK, HD), F32),
            pltpu.VMEM((BLOCK, HD), F32),
            pltpu.VMEM((BLOCK, HD), F32),
            pltpu.VMEM((QUARTER, HD), F32),
            pltpu.VMEM((QUARTER, HD), F32),
            pltpu.VMEM((QUARTER, HD), F32),
            pltpu.VMEM((16, 32, HD), BF16),
            pltpu.VMEM((16, 32, HD), BF16),
            pltpu.VMEM((16, 32, HD), BF16),
            pltpu.VMEM((4, QUARTER, BLOCK), BF16),
            pltpu.VMEM((2, QUARTER, half), BF16),
            pltpu.VMEM((2, QUARTER, half), BF16),
            pltpu.VMEM((2, QUARTER, half), BF16),
            pltpu.VMEM((2, QUARTER, half), BF16),
            pltpu.VMEM((2, QUARTER, half), BF16),
            pltpu.VMEM((2, QUARTER, half), BF16),
            pltpu.VMEM((QUARTER, part), F32),
            pltpu.VMEM((QUARTER, part), F32),
            pltpu.VMEM((QUARTER, part), F32),
            pltpu.VMEM((2, 64, half), BF16),
            pltpu.VMEM((2, 64, half), BF16),
            pltpu.SMEM((16,), jnp.int32),
            pltpu.SMEM((16,), jnp.int32),
            pltpu.SMEM((16,), jnp.int32),
            dma((4,)),
            dma((3,)),
            dma((4,)),
            dma((2,)),
            dma((2,)),
            dma((BACK + 1, 7)),
            dma((BACK + 1, 8)),
            dma((BACK, 2)),
            dma,
            dma((3,)),
            dma((4,)),
            dma((15,)),
            dma((16,)),
            dma((3,)),
            dma((4,)),
            dma((16,)),
            dma((16,)),
            pltpu.SemaphoreType.REGULAR,
            pltpu.SemaphoreType.REGULAR,
        ],
        compiler_params=pltpu.CompilerParams(collective_id=0, has_side_effects=True),
    )(lengths, page_table, norm_gain[None, :], freq, tokens, kv_weight, q_weight, out_weight)


def solution(mesh):
    half = HD // 2
    power = THETA ** (-np.arange(half, dtype=np.float64) * 2.0 / HD)
    freq = np.concatenate([power, power]).astype(np.float32)[None, :]
    placed = (
        P("seq", "narrow"),
        P("narrow"),
        P("narrow", "wide"),
        P("narrow", "wide"),
        P("wide", "narrow"),
        P(),
        P(),
    )

    def local(*args):
        return on_device(*args, jnp.asarray(freq))

    return jax.shard_map(
        local,
        mesh=mesh,
        in_specs=placed,
        out_specs=(P(("seq", "wide"), "narrow"), P("seq", None, "wide")),
        check_vma=False,
    )
```

```python
import jax
import jax.numpy as jnp
import numpy as np
from jax import lax
from jax.experimental import pallas as pl
from jax.experimental.pallas import tpu as pltpu
from jax.sharding import PartitionSpec as P

HEADS = 32
KV_HEADS = 4
HD = 128
WIDTH = 4096
BLOCK = 512
QUARTER = 128
EPS = 1e-05
THETA = 5000000.0
NEG = -1e30
BACK = 8
MESH = pl.DeviceIdType.MESH
F32 = jnp.float32
BF16 = jnp.bfloat16


def kernel(
    lens, table, gain, freq, tok_any, kvw_any, qw_any, ow_any,
    hid, cache,
    tok, kvw, qw, ow, scaled, kvp, kvr, qf, qs1, qr1, qs2, qr2, mykv,
    kv_all, queries, m_s, l_s, acc_s, cos_s, sin_s, rinv_s, pages, outg, inc,
    att, fxs, fxr, gps, gpr, gms, gmr, up, down, own, hss, hsr, order, slot_of, source,
    in_sem, a_send, a_recv, q_send, q_recv, kv_send, kv_recv, z_send, b_send,
    pg_send, pg_recv, ex_send, ex_recv, att_send, att_recv, o_send, o_recv, up_sem, down_sem,
):
    s = lax.axis_index("seq")
    w = lax.axis_index("wide")
    n = lax.axis_index("narrow")
    x, yh = lax.div(w, 2), lax.rem(w, 2)
    yl, k = lax.div(n, 2), lax.rem(n, 2)
    y = 2 * yh + yl

    def at_y(step):
        other = lax.rem(y + step, 4)
        return (s, 2 * x + lax.div(other, 2), 2 * lax.rem(other, 2) + k)

    def unit_y(step, core):
        return 2 * lax.rem(y + step, 4) + core

    partner = (s, w, 2 * yl + 1 - k)
    across = (s, w, 2 * (1 - yl) + k)

    def key_half(column):
        return lax.rem(lax.div(column + 1, 2) + 1, 2)

    home_half = lax.rem(key_half(lax.rem(w, 4)) + lax.div(w, 4), 2)
    home = 2 * lax.rem(w, 4) + home_half
    from_home = x + 4 * lax.rem(yh + key_half(x), 2)
    z_next = (lax.rem(s + 1, 16), w, n)
    z_prev = (lax.rem(s + 15, 16), w, n)
    z_jump = (lax.rem(s + 3, 16), w, n)
    z_back = (lax.rem(s + 13, 16), w, n)
    x_next = (s, 2 * lax.rem(x + 1, 4) + yh, n)
    x_prev = (s, 2 * lax.rem(x + 3, 4) + yh, n)
    y_far = (s, 2 * x + 1 - yh, n)

    def send(src, dst, send_sem, recv_sem, device):
        copy = pltpu.make_async_remote_copy(
            src_ref=src, dst_ref=dst, send_sem=send_sem, recv_sem=recv_sem,
            device_id=device, device_id_type=MESH,
        )
        copy.start()
        pending.append(copy)

    def arrived(dst, recv_sem):
        pltpu.make_async_remote_copy(
            src_ref=dst, dst_ref=dst, send_sem=q_send.at[0], recv_sem=recv_sem,
            device_id=partner, device_id_type=MESH,
        ).wait_recv()

    pending = []

    def quarter(q):
        return pl.ds(pl.multiple_of(q * QUARTER, QUARTER), QUARTER)

    turns = (lax.rem(n + 2, 4), 3 - n, 2 * yl + 1 - k, n)
    loads = []
    for number, (src, dst) in enumerate(
        [(kvw_any, kvw)]
        + [(tok_any.at[quarter(q), :], tok.at[quarter(q), :]) for q in turns]
        + [(qw_any, qw), (ow_any, ow)]
    ):
        load = pltpu.make_async_copy(src, dst, in_sem.at[number])
        loads.append(load)
    for load in loads[:5]:
        load.start()

    barrier = pltpu.get_barrier_semaphore()
    near = (
        [(s, w, lax.rem(n + step, 4)) for step in (1, 2, 3)]
        + [(s, home, n), (s, from_home, n), z_next, z_prev, z_jump, z_back, at_y(1), at_y(3), x_next, x_prev, y_far]
    )
    for device in near:
        pl.semaphore_signal(barrier, inc=1, device_id=device, device_id_type=MESH)

    loads[0].wait()
    for turn, q in enumerate(turns):
        loads[1 + turn].wait()
        if turn < 2:
            loads[5 + turn].start()
        rows = quarter(q)
        local = tok[rows, :].astype(F32)
        norm = jnp.sum(local * local, axis=1, keepdims=True)
        part = (local * gain[...]).astype(BF16)
        scaled[rows, :] = part
        kvp[q, 0:QUARTER, :] = jnp.dot(part, kvw[...], preferred_element_type=F32)
        turned = jnp.transpose(jnp.broadcast_to(norm, (QUARTER, QUARTER)))
        kvp[q, QUARTER:QUARTER + 8, :] = turned[0:8, :]
        if turn == 0:
            pl.semaphore_wait(barrier, len(near))
        if turn < 3:
            send(kvp.at[q], kvr.at[n], a_send.at[turn], a_recv.at[n], (s, w, q))

    def pass_on(first):
        if first != 1:
            pl.semaphore_wait(up_sem, 1)
            pl.semaphore_wait(down_sem, 1)
        if first < 2:
            pl.semaphore_signal(up_sem, inc=1, device_id=z_prev, device_id_type=MESH)
            pl.semaphore_signal(down_sem, inc=1, device_id=z_next, device_id_type=MESH)

    pass_on(1)

    loads[5].wait()
    for j in range(2):
        q = 2 * j + 1 - k
        rows = pl.ds(pl.multiple_of(q * QUARTER, QUARTER), QUARTER)
        qs1[j] = jnp.dot(scaled[rows, :], qw[...], preferred_element_type=F32).astype(BF16)
    send(qs1, qr1, q_send.at[0], q_recv.at[0], partner)

    index = (
        s * BLOCK + n * QUARTER
        + lax.broadcasted_iota(jnp.int32, (QUARTER, HD), 0)
    )
    end0 = lens[0]
    end1 = end0 + lens[1]
    end2 = end1 + lens[2]
    begin = jnp.where(index >= end0, end0, 0)
    begin = jnp.where(index >= end1, end1, begin)
    begin = jnp.where(index >= end2, end2, begin)
    angle = (index - begin).astype(F32) * freq[...]
    lane = lax.broadcasted_iota(jnp.int32, (QUARTER, HD), 1)
    cos_s[...] = jnp.cos(angle)
    sine = jnp.sin(angle)
    sin_s[...] = jnp.where(lane < HD // 2, -sine, sine)

    for step in (1, 2, 3):
        q = lax.rem(n + step, 4)
        arrived(kvr.at[q], a_recv.at[q])
    total = kvp[n] + kvr[lax.rem(n + 1, 4)] + kvr[lax.rem(n + 2, 4)] + kvr[lax.rem(n + 3, 4)]
    rinv = lax.rsqrt(total[QUARTER:QUARTER + 1, :] / WIDTH + EPS)
    rinv = jnp.transpose(jnp.broadcast_to(rinv, (QUARTER, QUARTER)))
    rinv_s[...] = rinv

    def rotate(values):
        return values * cos_s[...] + pltpu.roll(values, HD // 2, 1) * sin_s[...]

    plain = total[0:QUARTER, :] * rinv
    final = jnp.where(w < KV_HEADS, rotate(plain), plain).astype(BF16)
    mykv[...] = final
    pages[pl.ds(4 * n, 4)] = final.reshape(4, 32, HD)

    unit = unit_y(0, k)
    send(
        mykv, kv_all.at[0, 4 * home_half + n], b_send,
        kv_recv.at[0, 4 * home_half + n], (s, home, n),
    )

    for j in range(2):
        q = 2 * j + k
        rows = pl.ds(pl.multiple_of(q * QUARTER, QUARTER), QUARTER)
        qf[j] = jnp.dot(scaled[rows, :], qw[...], preferred_element_type=F32)
    arrived(qr1, q_recv.at[0])
    qs2[...] = (qf[1 - yl] + qr1[1 - yl].astype(F32)).astype(BF16)
    send(qs2, qr2, q_send.at[1], q_recv.at[1], across)

    def page_order():
        def owned(r, carry):
            found = jnp.int32(0)
            for j in range(16):
                owner = lax.shift_right_logical(table[16 * s + j], 4)
                found = jnp.where(owner == r, j, found)
            order[r] = found
            place = jnp.int32(0)
            for j in range(16):
                slot = table[16 * r + j]
                mine = lax.shift_right_logical(slot, 4) == s
                place = jnp.where(mine, slot & 15, place)
            slot_of[r] = place
            return carry

        lax.fori_loop(0, 16, owned, 0)

        def placed(slot, carry):
            found = jnp.int32(0)
            for j in range(16):
                found = jnp.where(slot_of[j] == slot, j, found)
            source[slot] = found
            return carry

        lax.fori_loop(0, 16, placed, 0)

    page_order()

    hops = {0: (1, 3), 1: (1,), 3: (1, 3), 4: (1,), 6: (1,), 7: (1,)}

    def piece_copy(block, action):
        step, target = ((0, at_y(1)), (0, at_y(3)), (0, partner), (None, at_y(1 + 2 * k)),
                        (1, partner), (3, partner), (2, partner))[action]
        piece = unit_y(3 + 2 * k if step is None else step, k)
        return pltpu.make_async_remote_copy(
            src_ref=kv_all.at[block, piece], dst_ref=kv_all.at[block, piece],
            send_sem=kv_send.at[block, action], recv_sem=kv_recv.at[block, piece],
            device_id=target, device_id_type=MESH,
        )

    def jump_copy(block, step):
        return pltpu.make_async_remote_copy(
            src_ref=kv_all.at[block, unit], dst_ref=kv_all.at[block + step, unit],
            send_sem=z_send.at[block, step // 2], recv_sem=kv_recv.at[block + step, unit],
            device_id=(lax.rem(s + step, 16), w, n), device_id_type=MESH,
        )

    def spread(block, *actions):
        for action in actions:
            piece_copy(block, action).start()

    def landed(block, piece):
        arrived(kv_all.at[block, piece], kv_recv.at[block, piece])

    def own_unit(block):
        landed(block, unit)
        for step in hops.get(block, ()):
            pl.when(s < 16 - step)(lambda step=step: jump_copy(block, step).start())
        spread(block, 0, 1, 2)

    def near_units(block):
        landed(block, unit_y(1, k))
        landed(block, unit_y(3, k))
        spread(block, 3, 4, 5)

    def far_unit(block):
        landed(block, unit_y(2, k))
        spread(block, 6)

    def settle(block):
        for step in hops.get(block, ()):
            pl.when(s < 16 - step)(lambda step=step: jump_copy(block, step).wait_send())
        for action in range(7):
            piece_copy(block, action).wait_send()

    def present(block, action):
        if block == 0:
            action(0)
        else:
            pl.when(s >= block)(lambda: action(block))

    scale = 1.0 / (HD ** 0.5 * float(np.log(2.0)))

    def attend(block):
        for step in range(4):
            landed(block, unit_y(step, 1 - k))
        keys = kv_all[block, pl.ds(4 * key_half(x), 4)].reshape(BLOCK, HD)
        values = kv_all[block, pl.ds(4 - 4 * key_half(x), 4)].reshape(BLOCK, HD)
        shape = (4, QUARTER, BLOCK)
        key_index = (s - block) * BLOCK + lax.broadcasted_iota(jnp.int32, shape, 2)
        row = s * BLOCK + n * QUARTER + lax.broadcasted_iota(jnp.int32, (4, QUARTER, 1), 1)
        first = jnp.where(row >= end0, end0, 0)
        first = jnp.where(row >= end1, end1, first)
        first = jnp.where(row >= end2, end2, first)
        allowed = key_index >= first
        if block == 0:
            allowed = allowed & (key_index <= row)
        scores = lax.dot_general(
            queries[...], keys, (((1,), (1,)), ((), ())), preferred_element_type=F32
        )
        masked = jnp.where(allowed.reshape(BLOCK, BLOCK), scores, NEG)
        top = jnp.broadcast_to(jnp.max(masked, axis=1, keepdims=True), (BLOCK, HD))
        if block > 0:
            old = m_s[...]
            top = jnp.maximum(old, top)
        weights = jnp.exp2((masked - jnp.concatenate([top] * 4, axis=1)) * scale)
        lanes = (weights[:, 0:HD] + weights[:, HD:2 * HD]) + (
            weights[:, 2 * HD:3 * HD] + weights[:, 3 * HD:]
        )
        mixed = jnp.dot(weights.astype(BF16), values, preferred_element_type=F32)
        if block > 0:
            alpha = jnp.exp2((old - top) * scale)
            lanes = l_s[...] * alpha + lanes
            mixed = acc_s[...] * alpha + mixed
        m_s[...] = top
        l_s[...] = lanes
        acc_s[...] = mixed

    def finish_queries():
        arrived(qr2, q_recv.at[1])
        summed = qf[yl] + qr1[yl].astype(F32) + qr2[...].astype(F32)
        for h in range(4):
            value = summed[:, h * HD:(h + 1) * HD] * rinv_s[...]
            queries[h * QUARTER:(h + 1) * QUARTER, :] = rotate(value).astype(BF16)

    def gather_pages():
        for step in (1, 2, 3):
            send(
                pages.at[pl.ds(4 * n, 4)], pages.at[pl.ds(4 * n, 4)],
                pg_send.at[step - 1], pg_recv.at[n], (s, w, lax.rem(n + step, 4)),
            )

    def pack_pages():
        for step in (1, 2, 3):
            q = lax.rem(n + step, 4)
            arrived(pages.at[pl.ds(4 * q, 4)], pg_recv.at[q])
        for r in range(16):
            outg[r] = pages[order[r]]
        inc[s] = outg[s]

    def send_pages():
        for step in (8, 7, 9, 6, 10, 5, 11, 4, 12, 3, 13, 2, 14, 1, 15):
            r = lax.rem(s + step, 16)
            send(outg.at[r], inc.at[s], ex_send.at[step - 1], ex_recv.at[s], (r, w, n))

    reach = {0: 0.0, 1: 2.4, 2: 4.8, 3: 3.9, 4: 6.3, 5: 8.7, 6: 7.8, 7: 10.2, 8: 12.6}
    events = [(6.7, 0, finish_queries, None), (7.0, 0, gather_pages, None),
              (12.9, 0, pack_pages, None), (13.0, 0, send_pages, None)]
    for level in range(8):
        events.append((2.0 + 1.4 * level, 1, pass_on, 0 if level < 7 else 2))
    for block, time in reach.items():
        events.append((time, 2, own_unit, block))
        events.append((time + 2.6, 3, near_units, block))
        events.append((time + 5.2, 4, far_unit, block))
        events.append((time + 6.8, 5, attend, block))
    for _, kind, action, value in sorted(events, key=lambda e: e[:2]):
        if kind == 0:
            action()
        elif kind == 1:
            action(value)
        else:
            present(value, action)

    mixed = acc_s[...] / jnp.sum(l_s[...], axis=1, keepdims=True)
    for h in range(4):
        att[n, :, h * HD:(h + 1) * HD] = mixed[h * QUARTER:(h + 1) * QUARTER].astype(BF16)
    send(att.at[n], att.at[n], att_send.at[0], att_recv.at[n], across)
    send(att.at[n], att.at[n], att_send.at[1], att_recv.at[n], partner)
    loads[6].wait()
    other = 2 * (1 - yl) + k
    arrived(att.at[other], att_recv.at[other])
    send(att.at[other], att.at[other], att_send.at[2], att_recv.at[other], partner)
    for q in (2 * yl + 1 - k, 2 * (1 - yl) + 1 - k):
        arrived(att.at[q], att_recv.at[q])

    def product(step):
        return jnp.dot(att[lax.rem(x + step, 4)], ow[...], preferred_element_type=F32)

    half = WIDTH // 8
    left, right = pl.ds(0, half), pl.ds(half, half)
    away = pl.ds(pl.multiple_of(64 * (1 - yh), 64), 64)
    mine = pl.ds(pl.multiple_of(64 * yh, 64), 64)

    def give(src, dst, part, rows, number, device):
        send(
            src.at[part, rows, :], dst.at[part, rows, :],
            o_send.at[number], o_recv.at[number], device,
        )

    def got(dst, part, rows, number):
        arrived(dst.at[part, rows, :], o_recv.at[number])

    far = product(2)
    fxs[0] = far[:, 0:half].astype(BF16)
    fxs[1] = far[:, half:].astype(BF16)
    give(fxs, fxr, 0, away, 0, x_next)
    give(fxs, fxr, 1, away, 1, x_prev)
    up[...] = product(1)
    gps[1] = up[:, right].astype(BF16)
    give(gps, gpr, 1, away, 2, x_next)
    down[...] = product(3)
    gms[0] = down[:, left].astype(BF16)
    give(gms, gmr, 0, away, 3, x_prev)
    give(fxs, fxr, 0, mine, 4, x_next)
    give(fxs, fxr, 1, mine, 5, x_prev)
    own[...] = product(0)
    for rows, number in ((away, 0), (mine, 4)):
        got(fxr, 0, rows, number)
        gps[0, rows, :] = (up[rows, left] + fxr[0, rows, :].astype(F32)).astype(BF16)
        give(gps, gpr, 0, rows, 8 + number, x_next)
        got(fxr, 1, rows, number + 1)
        gms[1, rows, :] = (down[rows, right] + fxr[1, rows, :].astype(F32)).astype(BF16)
        give(gms, gmr, 1, rows, 9 + number, x_prev)
        if number == 0:
            give(gps, gpr, 1, mine, 6, x_next)
            give(gms, gmr, 0, mine, 7, x_prev)

    def summed(rows, part):
        cols = pl.ds(part * half, half)
        return own[rows, cols] + gpr[part, rows, :].astype(F32) + gmr[part, rows, :].astype(F32)

    got(gpr, 1, away, 2)
    got(gmr, 1, away, 9)
    hss[1] = summed(away, 1).astype(BF16)
    send(hss.at[1], hsr.at[1], o_send.at[15], o_recv.at[15], y_far)
    got(gmr, 0, away, 3)
    got(gpr, 0, away, 8)
    hss[0] = summed(away, 0).astype(BF16)
    send(hss.at[0], hsr.at[0], o_send.at[14], o_recv.at[14], y_far)

    for step in range(1, 16):
        r = lax.rem(s + step, 16)
        arrived(inc.at[r], ex_recv.at[r])
    for slot in range(16):
        cache[slot] = inc[source[slot]]

    got(gpr, 1, mine, 6)
    got(gmr, 0, mine, 7)
    got(gpr, 0, mine, 12)
    got(gmr, 1, mine, 13)
    rows = pl.ds(pl.multiple_of(64 * w, 64), 64)
    for part in (1, 0):
        cols = pl.ds(part * half, half)
        base = tok[rows, cols].astype(F32) + summed(mine, part)
        arrived(hsr.at[part], o_recv.at[14 + part])
        hid[:, cols] = (base + hsr[part].astype(F32)).astype(BF16)

    for copy in pending:
        copy.wait_send()
    for block in range(BACK + 1):
        present(block, settle)


def on_device(tokens, norm_gain, q_weight, kv_weight, out_weight, lengths, page_table, freq):
    vmem = pl.BlockSpec(memory_space=pltpu.VMEM)
    smem = pl.BlockSpec(memory_space=pltpu.SMEM)
    hbm = pl.BlockSpec(memory_space=pl.ANY)
    dma = pltpu.SemaphoreType.DMA
    part = WIDTH // 4
    half = part // 2
    return pl.pallas_call(
        kernel,
        out_shape=(
            pltpu.VMEM((64, part), BF16),
            pltpu.VMEM((16, 32, HD), BF16),
        ),
        in_specs=[smem, smem, vmem, vmem, hbm, hbm, hbm, hbm],
        out_specs=(vmem, vmem),
        scratch_shapes=[
            pltpu.VMEM((BLOCK, part), BF16),
            pltpu.VMEM((part, HD), BF16),
            pltpu.VMEM((part, BLOCK), BF16),
            pltpu.VMEM((BLOCK, part), BF16),
            pltpu.VMEM((BLOCK, part), BF16),
            pltpu.VMEM((4, QUARTER + 8, HD), F32),
            pltpu.VMEM((4, QUARTER + 8, HD), F32),
            pltpu.VMEM((2, QUARTER, BLOCK), F32),
            pltpu.VMEM((2, QUARTER, BLOCK), BF16),
            pltpu.VMEM((2, QUARTER, BLOCK), BF16),
            pltpu.VMEM((QUARTER, BLOCK), BF16),
            pltpu.VMEM((QUARTER, BLOCK), BF16),
            pltpu.VMEM((QUARTER, HD), BF16),
            pltpu.VMEM((BACK + 1, 8, QUARTER, HD), BF16),
            pltpu.VMEM((BLOCK, HD), BF16),
            pltpu.VMEM((BLOCK, HD), F32),
            pltpu.VMEM((BLOCK, HD), F32),
            pltpu.VMEM((BLOCK, HD), F32),
            pltpu.VMEM((QUARTER, HD), F32),
            pltpu.VMEM((QUARTER, HD), F32),
            pltpu.VMEM((QUARTER, HD), F32),
            pltpu.VMEM((16, 32, HD), BF16),
            pltpu.VMEM((16, 32, HD), BF16),
            pltpu.VMEM((16, 32, HD), BF16),
            pltpu.VMEM((4, QUARTER, BLOCK), BF16),
            pltpu.VMEM((2, QUARTER, half), BF16),
            pltpu.VMEM((2, QUARTER, half), BF16),
            pltpu.VMEM((2, QUARTER, half), BF16),
            pltpu.VMEM((2, QUARTER, half), BF16),
            pltpu.VMEM((2, QUARTER, half), BF16),
            pltpu.VMEM((2, QUARTER, half), BF16),
            pltpu.VMEM((QUARTER, part), F32),
            pltpu.VMEM((QUARTER, part), F32),
            pltpu.VMEM((QUARTER, part), F32),
            pltpu.VMEM((2, 64, half), BF16),
            pltpu.VMEM((2, 64, half), BF16),
            pltpu.SMEM((16,), jnp.int32),
            pltpu.SMEM((16,), jnp.int32),
            pltpu.SMEM((16,), jnp.int32),
            dma((7,)),
            dma((3,)),
            dma((4,)),
            dma((2,)),
            dma((2,)),
            dma((BACK + 1, 7)),
            dma((BACK + 1, 8)),
            dma((BACK, 2)),
            dma,
            dma((3,)),
            dma((4,)),
            dma((15,)),
            dma((16,)),
            dma((3,)),
            dma((4,)),
            dma((16,)),
            dma((16,)),
            pltpu.SemaphoreType.REGULAR,
            pltpu.SemaphoreType.REGULAR,
        ],
        compiler_params=pltpu.CompilerParams(collective_id=0, has_side_effects=True),
    )(lengths, page_table, norm_gain[None, :], freq, tokens, kv_weight, q_weight, out_weight)


def solution(mesh):
    half = HD // 2
    power = THETA ** (-np.arange(half, dtype=np.float64) * 2.0 / HD)
    freq = np.concatenate([power, power]).astype(np.float32)[None, :]
    placed = (
        P("seq", "narrow"),
        P("narrow"),
        P("narrow", "wide"),
        P("narrow", "wide"),
        P("wide", "narrow"),
        P(),
        P(),
    )

    def local(*args):
        return on_device(*args, jnp.asarray(freq))

    return jax.shard_map(
        local,
        mesh=mesh,
        in_specs=placed,
        out_specs=(P(("seq", "wide"), "narrow"), P("seq", None, "wide")),
        check_vma=False,
    )
```

```python
import jax
import jax.numpy as jnp
import numpy as np
from jax import lax
from jax.experimental import pallas as pl
from jax.experimental.pallas import tpu as pltpu
from jax.sharding import PartitionSpec as P

HEADS = 32
KV_HEADS = 4
HD = 128
WIDTH = 4096
BLOCK = 512
QUARTER = 128
EPS = 1e-05
THETA = 5000000.0
NEG = -1e30
BACK = 8
MESH = pl.DeviceIdType.MESH
F32 = jnp.float32
BF16 = jnp.bfloat16


def kernel(
    lens, table, gain, freq, tok_any, kvw_any, qw_any, ow_any,
    hid, cache,
    tok, kvw, qw, ow, scaled, kvp, kvr, qf, qs1, qr1, qs2, qr2, mykv,
    kv_all, queries, m_s, l_s, acc_s, cos_s, sin_s, rinv_s, pages, outg, inc,
    att, fxs, fxr, gps, gpr, gms, gmr, up, down, own, hss, hsr, order, slot_of, source,
    in_sem, a_send, a_recv, q_send, q_recv, kv_send, kv_recv, z_send, b_send,
    pg_send, pg_recv, ex_send, ex_recv, att_send, att_recv, o_send, o_recv, up_sem, down_sem,
):
    s = lax.axis_index("seq")
    w = lax.axis_index("wide")
    n = lax.axis_index("narrow")
    x, yh = lax.div(w, 2), lax.rem(w, 2)
    yl, k = lax.div(n, 2), lax.rem(n, 2)
    y = 2 * yh + yl

    def at_y(step):
        other = lax.rem(y + step, 4)
        return (s, 2 * x + lax.div(other, 2), 2 * lax.rem(other, 2) + k)

    def unit_y(step, core):
        return 2 * lax.rem(y + step, 4) + core

    partner = (s, w, 2 * yl + 1 - k)
    across = (s, w, 2 * (1 - yl) + k)

    def key_half(column):
        return lax.rem(lax.div(column + 1, 2) + 1, 2)

    home_half = lax.rem(key_half(lax.rem(w, 4)) + lax.div(w, 4), 2)
    home = 2 * lax.rem(w, 4) + home_half
    from_home = x + 4 * lax.rem(yh + key_half(x), 2)
    z_next = (lax.rem(s + 1, 16), w, n)
    z_prev = (lax.rem(s + 15, 16), w, n)
    z_jump = (lax.rem(s + 3, 16), w, n)
    z_back = (lax.rem(s + 13, 16), w, n)
    x_next = (s, 2 * lax.rem(x + 1, 4) + yh, n)
    x_prev = (s, 2 * lax.rem(x + 3, 4) + yh, n)
    y_far = (s, 2 * x + 1 - yh, n)

    def send(src, dst, send_sem, recv_sem, device):
        copy = pltpu.make_async_remote_copy(
            src_ref=src, dst_ref=dst, send_sem=send_sem, recv_sem=recv_sem,
            device_id=device, device_id_type=MESH,
        )
        copy.start()
        pending.append(copy)

    def arrived(dst, recv_sem):
        pltpu.make_async_remote_copy(
            src_ref=dst, dst_ref=dst, send_sem=q_send.at[0], recv_sem=recv_sem,
            device_id=partner, device_id_type=MESH,
        ).wait_recv()

    pending = []

    def quarter(q):
        return pl.ds(pl.multiple_of(q * QUARTER, QUARTER), QUARTER)

    turns = (lax.rem(n + 2, 4), 3 - n, 2 * yl + 1 - k, n)
    loads = []
    for number, (src, dst) in enumerate(
        [(kvw_any, kvw)]
        + [(tok_any.at[quarter(q), :], tok.at[quarter(q), :]) for q in turns]
        + [(qw_any, qw), (ow_any, ow)]
    ):
        load = pltpu.make_async_copy(src, dst, in_sem.at[number])
        loads.append(load)
    for load in loads[:5]:
        load.start()

    barrier = pltpu.get_barrier_semaphore()
    near = (
        [(s, w, lax.rem(n + step, 4)) for step in (1, 2, 3)]
        + [(s, home, n), (s, from_home, n), z_next, z_prev, z_jump, z_back, at_y(1), at_y(3), x_next, x_prev, y_far]
    )
    for device in near:
        pl.semaphore_signal(barrier, inc=1, device_id=device, device_id_type=MESH)

    loads[0].wait()
    for turn, q in enumerate(turns):
        loads[1 + turn].wait()
        if turn < 2:
            loads[5 + turn].start()
        rows = quarter(q)
        local = tok[rows, :].astype(F32)
        norm = jnp.sum(local * local, axis=1, keepdims=True)
        part = (local * gain[...]).astype(BF16)
        scaled[rows, :] = part
        kvp[q, 0:QUARTER, :] = jnp.dot(part, kvw[...], preferred_element_type=F32)
        turned = jnp.transpose(jnp.broadcast_to(norm, (QUARTER, QUARTER)))
        kvp[q, QUARTER:QUARTER + 8, :] = turned[0:8, :]
        if turn == 0:
            pl.semaphore_wait(barrier, len(near))
        if turn < 3:
            send(kvp.at[q], kvr.at[n], a_send.at[turn], a_recv.at[n], (s, w, q))

    def pass_on(first):
        if first != 1:
            pl.semaphore_wait(up_sem, 1)
            pl.semaphore_wait(down_sem, 1)
        if first < 2:
            pl.semaphore_signal(up_sem, inc=1, device_id=z_prev, device_id_type=MESH)
            pl.semaphore_signal(down_sem, inc=1, device_id=z_next, device_id_type=MESH)

    pass_on(1)

    loads[5].wait()
    for j in range(2):
        q = 2 * j + 1 - k
        rows = pl.ds(pl.multiple_of(q * QUARTER, QUARTER), QUARTER)
        qs1[j] = jnp.dot(scaled[rows, :], qw[...], preferred_element_type=F32).astype(BF16)
    send(qs1, qr1, q_send.at[0], q_recv.at[0], partner)

    index = (
        s * BLOCK + n * QUARTER
        + lax.broadcasted_iota(jnp.int32, (QUARTER, HD), 0)
    )
    end0 = lens[0]
    end1 = end0 + lens[1]
    end2 = end1 + lens[2]
    begin = jnp.where(index >= end0, end0, 0)
    begin = jnp.where(index >= end1, end1, begin)
    begin = jnp.where(index >= end2, end2, begin)
    angle = (index - begin).astype(F32) * freq[...]
    lane = lax.broadcasted_iota(jnp.int32, (QUARTER, HD), 1)
    cos_s[...] = jnp.cos(angle)
    sine = jnp.sin(angle)
    sin_s[...] = jnp.where(lane < HD // 2, -sine, sine)

    for step in (1, 2, 3):
        q = lax.rem(n + step, 4)
        arrived(kvr.at[q], a_recv.at[q])
    total = kvp[n] + kvr[lax.rem(n + 1, 4)] + kvr[lax.rem(n + 2, 4)] + kvr[lax.rem(n + 3, 4)]
    rinv = lax.rsqrt(total[QUARTER:QUARTER + 1, :] / WIDTH + EPS)
    rinv = jnp.transpose(jnp.broadcast_to(rinv, (QUARTER, QUARTER)))
    rinv_s[...] = rinv

    def rotate(values):
        return values * cos_s[...] + pltpu.roll(values, HD // 2, 1) * sin_s[...]

    plain = total[0:QUARTER, :] * rinv
    final = jnp.where(w < KV_HEADS, rotate(plain), plain).astype(BF16)
    mykv[...] = final
    pages[pl.ds(4 * n, 4)] = final.reshape(4, 32, HD)

    unit = unit_y(0, k)
    send(
        mykv, kv_all.at[0, 4 * home_half + n], b_send,
        kv_recv.at[0, 4 * home_half + n], (s, home, n),
    )

    for j in range(2):
        q = 2 * j + k
        rows = pl.ds(pl.multiple_of(q * QUARTER, QUARTER), QUARTER)
        qf[j] = jnp.dot(scaled[rows, :], qw[...], preferred_element_type=F32)
    arrived(qr1, q_recv.at[0])
    qs2[...] = (qf[1 - yl] + qr1[1 - yl].astype(F32)).astype(BF16)
    send(qs2, qr2, q_send.at[1], q_recv.at[1], across)

    def page_order():
        def owned(r, carry):
            found = jnp.int32(0)
            for j in range(16):
                owner = lax.shift_right_logical(table[16 * s + j], 4)
                found = jnp.where(owner == r, j, found)
            order[r] = found
            place = jnp.int32(0)
            for j in range(16):
                slot = table[16 * r + j]
                mine = lax.shift_right_logical(slot, 4) == s
                place = jnp.where(mine, slot & 15, place)
            slot_of[r] = place
            return carry

        lax.fori_loop(0, 16, owned, 0)

        def placed(slot, carry):
            found = jnp.int32(0)
            for j in range(16):
                found = jnp.where(slot_of[j] == slot, j, found)
            source[slot] = found
            return carry

        lax.fori_loop(0, 16, placed, 0)

    page_order()

    straight = (7, 8)
    hops = {0: (1, 3), 1: (1,), 3: (1, 3), 4: (1,), 6: (1,), 7: (1,)}

    def piece_copy(block, action):
        step, target = ((0, at_y(1)), (0, at_y(3)), (0, partner), (None, at_y(1 + 2 * k)),
                        (1, partner), (3, partner), (2, partner), (0, y_far))[action]
        piece = unit_y(3 + 2 * k if step is None else step, k)
        return pltpu.make_async_remote_copy(
            src_ref=kv_all.at[block, piece], dst_ref=kv_all.at[block, piece],
            send_sem=kv_send.at[block, min(action, 3) if action == 7 else action], recv_sem=kv_recv.at[block, piece],
            device_id=target, device_id_type=MESH,
        )

    def jump_copy(block, step):
        return pltpu.make_async_remote_copy(
            src_ref=kv_all.at[block, unit], dst_ref=kv_all.at[block + step, unit],
            send_sem=z_send.at[block, step // 2], recv_sem=kv_recv.at[block + step, unit],
            device_id=(lax.rem(s + step, 16), w, n), device_id_type=MESH,
        )

    def spread(block, *actions):
        for action in actions:
            piece_copy(block, action).start()

    def landed(block, piece):
        arrived(kv_all.at[block, piece], kv_recv.at[block, piece])

    def own_unit(block):
        landed(block, unit)
        for step in hops.get(block, ()):
            pl.when(s < 16 - step)(lambda step=step: jump_copy(block, step).start())
        spread(block, 0, 1, 2)
        if block in straight:
            spread(block, 7)

    def near_units(block):
        landed(block, unit_y(1, k))
        landed(block, unit_y(3, k))
        spread(block, *((4, 5) if block in straight else (3, 4, 5)))

    def far_unit(block):
        landed(block, unit_y(2, k))
        spread(block, 6)

    def settle(block):
        for step in hops.get(block, ()):
            pl.when(s < 16 - step)(lambda step=step: jump_copy(block, step).wait_send())
        for action in (0, 1, 2, 7 if block in straight else 3, 4, 5, 6):
            piece_copy(block, action).wait_send()

    def present(block, action):
        if block == 0:
            action(0)
        else:
            pl.when(s >= block)(lambda: action(block))

    scale = 1.0 / (HD ** 0.5 * float(np.log(2.0)))

    def attend(block):
        for step in range(4):
            landed(block, unit_y(step, 1 - k))
        keys = kv_all[block, pl.ds(4 * key_half(x), 4)].reshape(BLOCK, HD)
        values = kv_all[block, pl.ds(4 - 4 * key_half(x), 4)].reshape(BLOCK, HD)
        shape = (4, QUARTER, BLOCK)
        key_index = (s - block) * BLOCK + lax.broadcasted_iota(jnp.int32, shape, 2)
        row = s * BLOCK + n * QUARTER + lax.broadcasted_iota(jnp.int32, (4, QUARTER, 1), 1)
        first = jnp.where(row >= end0, end0, 0)
        first = jnp.where(row >= end1, end1, first)
        first = jnp.where(row >= end2, end2, first)
        allowed = key_index >= first
        if block == 0:
            allowed = allowed & (key_index <= row)
        scores = lax.dot_general(
            queries[...], keys, (((1,), (1,)), ((), ())), preferred_element_type=F32
        )
        masked = jnp.where(allowed.reshape(BLOCK, BLOCK), scores, NEG)
        top = jnp.broadcast_to(jnp.max(masked, axis=1, keepdims=True), (BLOCK, HD))
        if block > 0:
            old = m_s[...]
            top = jnp.maximum(old, top)
        weights = jnp.exp2((masked - jnp.concatenate([top] * 4, axis=1)) * scale)
        lanes = (weights[:, 0:HD] + weights[:, HD:2 * HD]) + (
            weights[:, 2 * HD:3 * HD] + weights[:, 3 * HD:]
        )
        mixed = jnp.dot(weights.astype(BF16), values, preferred_element_type=F32)
        if block > 0:
            alpha = jnp.exp2((old - top) * scale)
            lanes = l_s[...] * alpha + lanes
            mixed = acc_s[...] * alpha + mixed
        m_s[...] = top
        l_s[...] = lanes
        acc_s[...] = mixed

    def finish_queries():
        arrived(qr2, q_recv.at[1])
        summed = qf[yl] + qr1[yl].astype(F32) + qr2[...].astype(F32)
        for h in range(4):
            value = summed[:, h * HD:(h + 1) * HD] * rinv_s[...]
            queries[h * QUARTER:(h + 1) * QUARTER, :] = rotate(value).astype(BF16)

    def gather_pages():
        for step in (1, 2, 3):
            send(
                pages.at[pl.ds(4 * n, 4)], pages.at[pl.ds(4 * n, 4)],
                pg_send.at[step - 1], pg_recv.at[n], (s, w, lax.rem(n + step, 4)),
            )

    def pack_pages():
        for step in (1, 2, 3):
            q = lax.rem(n + step, 4)
            arrived(pages.at[pl.ds(4 * q, 4)], pg_recv.at[q])
        for r in range(16):
            outg[r] = pages[order[r]]
        inc[s] = outg[s]

    def send_pages():
        for step in (8, 7, 9, 6, 10, 5, 11, 4, 12, 3, 13, 2, 14, 1, 15):
            r = lax.rem(s + step, 16)
            send(outg.at[r], inc.at[s], ex_send.at[step - 1], ex_recv.at[s], (r, w, n))

    reach = {0: 0.0, 1: 2.4, 2: 4.8, 3: 3.9, 4: 6.3, 5: 8.7, 6: 7.8, 7: 10.2, 8: 12.6}
    events = [(6.7, 0, finish_queries, None), (7.0, 0, gather_pages, None),
              (12.9, 0, pack_pages, None), (13.0, 0, send_pages, None)]
    for level in range(8):
        events.append((2.0 + 1.4 * level, 1, pass_on, 0 if level < 7 else 2))
    for block, time in reach.items():
        events.append((time, 2, own_unit, block))
        events.append((time + 2.6, 3, near_units, block))
        soon = 1.6 if block in straight else 0.0
        events.append((time + 5.2 - soon, 4, far_unit, block))
        events.append((time + 6.8 - soon, 5, attend, block))
    for _, kind, action, value in sorted(events, key=lambda e: e[:2]):
        if kind == 0:
            action()
        elif kind == 1:
            action(value)
        else:
            present(value, action)

    mixed = acc_s[...] / jnp.sum(l_s[...], axis=1, keepdims=True)
    for h in range(4):
        att[n, :, h * HD:(h + 1) * HD] = mixed[h * QUARTER:(h + 1) * QUARTER].astype(BF16)
    halves = (pl.ds(0, 64), pl.ds(64, 64))

    def share(q, part, number, device):
        piece = att.at[q, halves[part], :]
        send(piece, piece, att_send.at[number + part], att_recv.at[q, part], device)

    def shared(q, part):
        arrived(att.at[q, halves[part], :], att_recv.at[q, part])

    for part in range(2):
        share(n, part, 0, across)
    for part in range(2):
        share(n, part, 2, partner)
    loads[6].wait()
    other = 2 * (1 - yl) + k
    for part in range(2):
        shared(other, part)
        share(other, part, 4, partner)
    for q in (2 * yl + 1 - k, 2 * (1 - yl) + 1 - k):
        for part in range(2):
            shared(q, part)

    def product(step):
        return jnp.dot(att[lax.rem(x + step, 4)], ow[...], preferred_element_type=F32)

    half = WIDTH // 8
    left, right = pl.ds(0, half), pl.ds(half, half)
    starts = (64 * (1 - yh), 64 * (1 - yh) + 32, 64 * yh, 64 * yh + 32)
    chunks = [pl.ds(pl.multiple_of(start, 32), 32) for start in starts]
    routes = (
        (fxs, fxr, 0, x_next), (fxs, fxr, 1, x_prev), (gps, gpr, 1, x_next),
        (gms, gmr, 0, x_prev), (gps, gpr, 0, x_next), (gms, gmr, 1, x_prev),
    )

    def give(route, c):
        src, dst, part, device = routes[route]
        send(
            src.at[part, chunks[c], :], dst.at[part, chunks[c], :],
            o_send.at[6 * c + route], o_recv.at[6 * c + route], device,
        )

    def got(route, c):
        _, dst, part, _ = routes[route]
        arrived(dst.at[part, chunks[c], :], o_recv.at[6 * c + route])

    def relay(c):
        rows = chunks[c]
        got(0, c)
        gps[0, rows, :] = (up[rows, left] + fxr[0, rows, :].astype(F32)).astype(BF16)
        give(4, c)
        got(1, c)
        gms[1, rows, :] = (down[rows, right] + fxr[1, rows, :].astype(F32)).astype(BF16)
        give(5, c)

    def summed(c, part):
        rows = chunks[c]
        cols = pl.ds(part * half, half)
        return own[rows, cols] + gpr[part, rows, :].astype(F32) + gmr[part, rows, :].astype(F32)

    def pair(c):
        rows = pl.ds(32 * c, 32)
        for route in (2, 3, 4, 5):
            got(route, c)
        for part in range(2):
            hss[part, rows, :] = summed(c, part).astype(BF16)
            send(
                hss.at[part, rows, :], hsr.at[part, rows, :],
                o_send.at[24 + 2 * c + part], o_recv.at[24 + 2 * c + part], y_far,
            )

    far = product(2)
    fxs[0] = far[:, 0:half].astype(BF16)
    fxs[1] = far[:, half:].astype(BF16)
    give(0, 0)
    give(1, 0)
    up[...] = product(1)
    gps[1] = up[:, right].astype(BF16)
    give(2, 0)
    down[...] = product(3)
    gms[0] = down[:, left].astype(BF16)
    give(3, 0)
    give(0, 1)
    give(1, 1)
    own[...] = product(0)
    relay(0)
    give(2, 1)
    give(3, 1)
    give(0, 2)
    give(1, 2)
    relay(1)
    give(2, 2)
    give(3, 2)
    give(0, 3)
    give(1, 3)
    pair(0)
    relay(2)
    give(2, 3)
    give(3, 3)
    pair(1)
    relay(3)

    for step in range(1, 16):
        r = lax.rem(s + step, 16)
        arrived(inc.at[r], ex_recv.at[r])
    for slot in range(16):
        cache[slot] = inc[source[slot]]

    for c in range(2):
        for route in (2, 3, 4, 5):
            got(route, 2 + c)
        place = pl.ds(pl.multiple_of(64 * w + 32 * c, 32), 32)
        rows = pl.ds(32 * c, 32)
        for part in range(2):
            cols = pl.ds(part * half, half)
            base = tok[place, cols].astype(F32) + summed(2 + c, part)
            arrived(hsr.at[part, rows, :], o_recv.at[24 + 2 * c + part])
            hid[rows, cols] = (base + hsr[part, rows, :].astype(F32)).astype(BF16)

    for copy in pending:
        copy.wait_send()
    for block in range(BACK + 1):
        present(block, settle)


def on_device(tokens, norm_gain, q_weight, kv_weight, out_weight, lengths, page_table, freq):
    vmem = pl.BlockSpec(memory_space=pltpu.VMEM)
    smem = pl.BlockSpec(memory_space=pltpu.SMEM)
    hbm = pl.BlockSpec(memory_space=pl.ANY)
    dma = pltpu.SemaphoreType.DMA
    part = WIDTH // 4
    half = part // 2
    return pl.pallas_call(
        kernel,
        out_shape=(
            pltpu.VMEM((64, part), BF16),
            pltpu.VMEM((16, 32, HD), BF16),
        ),
        in_specs=[smem, smem, vmem, vmem, hbm, hbm, hbm, hbm],
        out_specs=(vmem, vmem),
        scratch_shapes=[
            pltpu.VMEM((BLOCK, part), BF16),
            pltpu.VMEM((part, HD), BF16),
            pltpu.VMEM((part, BLOCK), BF16),
            pltpu.VMEM((BLOCK, part), BF16),
            pltpu.VMEM((BLOCK, part), BF16),
            pltpu.VMEM((4, QUARTER + 8, HD), F32),
            pltpu.VMEM((4, QUARTER + 8, HD), F32),
            pltpu.VMEM((2, QUARTER, BLOCK), F32),
            pltpu.VMEM((2, QUARTER, BLOCK), BF16),
            pltpu.VMEM((2, QUARTER, BLOCK), BF16),
            pltpu.VMEM((QUARTER, BLOCK), BF16),
            pltpu.VMEM((QUARTER, BLOCK), BF16),
            pltpu.VMEM((QUARTER, HD), BF16),
            pltpu.VMEM((BACK + 1, 8, QUARTER, HD), BF16),
            pltpu.VMEM((BLOCK, HD), BF16),
            pltpu.VMEM((BLOCK, HD), F32),
            pltpu.VMEM((BLOCK, HD), F32),
            pltpu.VMEM((BLOCK, HD), F32),
            pltpu.VMEM((QUARTER, HD), F32),
            pltpu.VMEM((QUARTER, HD), F32),
            pltpu.VMEM((QUARTER, HD), F32),
            pltpu.VMEM((16, 32, HD), BF16),
            pltpu.VMEM((16, 32, HD), BF16),
            pltpu.VMEM((16, 32, HD), BF16),
            pltpu.VMEM((4, QUARTER, BLOCK), BF16),
            pltpu.VMEM((2, QUARTER, half), BF16),
            pltpu.VMEM((2, QUARTER, half), BF16),
            pltpu.VMEM((2, QUARTER, half), BF16),
            pltpu.VMEM((2, QUARTER, half), BF16),
            pltpu.VMEM((2, QUARTER, half), BF16),
            pltpu.VMEM((2, QUARTER, half), BF16),
            pltpu.VMEM((QUARTER, part), F32),
            pltpu.VMEM((QUARTER, part), F32),
            pltpu.VMEM((QUARTER, part), F32),
            pltpu.VMEM((2, 64, half), BF16),
            pltpu.VMEM((2, 64, half), BF16),
            pltpu.SMEM((16,), jnp.int32),
            pltpu.SMEM((16,), jnp.int32),
            pltpu.SMEM((16,), jnp.int32),
            dma((7,)),
            dma((3,)),
            dma((4,)),
            dma((2,)),
            dma((2,)),
            dma((BACK + 1, 7)),
            dma((BACK + 1, 8)),
            dma((BACK, 2)),
            dma,
            dma((3,)),
            dma((4,)),
            dma((15,)),
            dma((16,)),
            dma((6,)),
            dma((4, 2)),
            dma((28,)),
            dma((28,)),
            pltpu.SemaphoreType.REGULAR,
            pltpu.SemaphoreType.REGULAR,
        ],
        compiler_params=pltpu.CompilerParams(collective_id=0, has_side_effects=True),
    )(lengths, page_table, norm_gain[None, :], freq, tokens, kv_weight, q_weight, out_weight)


def solution(mesh):
    half = HD // 2
    power = THETA ** (-np.arange(half, dtype=np.float64) * 2.0 / HD)
    freq = np.concatenate([power, power]).astype(np.float32)[None, :]
    placed = (
        P("seq", "narrow"),
        P("narrow"),
        P("narrow", "wide"),
        P("narrow", "wide"),
        P("wide", "narrow"),
        P(),
        P(),
    )

    def local(*args):
        return on_device(*args, jnp.asarray(freq))

    return jax.shard_map(
        local,
        mesh=mesh,
        in_specs=placed,
        out_specs=(P(("seq", "wide"), "narrow"), P("seq", None, "wide")),
        check_vma=False,
    )
```

```python
import jax
import jax.numpy as jnp
import numpy as np
from jax import lax
from jax.experimental import pallas as pl
from jax.experimental.pallas import tpu as pltpu
from jax.sharding import PartitionSpec as P

HEADS = 32
KV_HEADS = 4
HD = 128
WIDTH = 4096
BLOCK = 512
QUARTER = 128
EPS = 1e-05
THETA = 5000000.0
NEG = -1e30
BACK = 8
MESH = pl.DeviceIdType.MESH
F32 = jnp.float32
BF16 = jnp.bfloat16


def kernel(
    lens, table, gain, freq, tok_any, kvw_any, qw_any, ow_any,
    hid, cache,
    tok, kvw, qw, ow, scaled, kvp, kvr, qf, qs1, qr1, qs2, qr2, mykv,
    kv_all, queries, m_s, l_s, acc_s, cos_s, sin_s, rinv_s, pages, outg, inc,
    att, fxs, fxr, gps, gpr, gms, gmr, up, down, own, hss, hsr, order, slot_of, source,
    in_sem, a_send, a_recv, q_send, q_recv, kv_send, kv_recv, z_send, b_send,
    pg_send, pg_recv, ex_send, ex_recv, att_send, att_recv, o_send, o_recv, up_sem, down_sem,
):
    s = lax.axis_index("seq")
    w = lax.axis_index("wide")
    n = lax.axis_index("narrow")
    x, yh = lax.div(w, 2), lax.rem(w, 2)
    yl, k = lax.div(n, 2), lax.rem(n, 2)
    y = 2 * yh + yl

    def at_y(step):
        other = lax.rem(y + step, 4)
        return (s, 2 * x + lax.div(other, 2), 2 * lax.rem(other, 2) + k)

    def unit_y(step, core):
        return 2 * lax.rem(y + step, 4) + core

    partner = (s, w, 2 * yl + 1 - k)
    across = (s, w, 2 * (1 - yl) + k)

    def key_half(column):
        return lax.rem(lax.div(column + 1, 2) + 1, 2)

    home_half = lax.rem(key_half(lax.rem(w, 4)) + lax.div(w, 4), 2)
    home = 2 * lax.rem(w, 4) + home_half
    from_home = x + 4 * lax.rem(yh + key_half(x), 2)
    z_next = (lax.rem(s + 1, 16), w, n)
    z_prev = (lax.rem(s + 15, 16), w, n)
    z_jump = (lax.rem(s + 3, 16), w, n)
    z_back = (lax.rem(s + 13, 16), w, n)
    x_next = (s, 2 * lax.rem(x + 1, 4) + yh, n)
    x_prev = (s, 2 * lax.rem(x + 3, 4) + yh, n)
    y_far = (s, 2 * x + 1 - yh, n)

    def send(src, dst, send_sem, recv_sem, device):
        copy = pltpu.make_async_remote_copy(
            src_ref=src, dst_ref=dst, send_sem=send_sem, recv_sem=recv_sem,
            device_id=device, device_id_type=MESH,
        )
        copy.start()
        pending.append(copy)

    def arrived(dst, recv_sem):
        pltpu.make_async_remote_copy(
            src_ref=dst, dst_ref=dst, send_sem=q_send.at[0], recv_sem=recv_sem,
            device_id=partner, device_id_type=MESH,
        ).wait_recv()

    pending = []

    def quarter(q):
        return pl.ds(pl.multiple_of(q * QUARTER, QUARTER), QUARTER)

    turns = (lax.rem(n + 2, 4), 3 - n, 2 * yl + 1 - k, n)
    loads = []
    for number, (src, dst) in enumerate(
        [(kvw_any, kvw)]
        + [(tok_any.at[quarter(q), :], tok.at[quarter(q), :]) for q in turns]
        + [(qw_any, qw), (ow_any, ow)]
    ):
        load = pltpu.make_async_copy(src, dst, in_sem.at[number])
        loads.append(load)
    for load in loads[:5]:
        load.start()

    barrier = pltpu.get_barrier_semaphore()
    near = (
        [(s, w, lax.rem(n + step, 4)) for step in (1, 2, 3)]
        + [(s, home, n), (s, from_home, n), z_next, z_prev, z_jump, z_back, at_y(1), at_y(3), x_next, x_prev, y_far]
    )
    for device in near:
        pl.semaphore_signal(barrier, inc=1, device_id=device, device_id_type=MESH)

    def page_order():
        def owned(r, carry):
            found = jnp.int32(0)
            for j in range(16):
                owner = lax.shift_right_logical(table[16 * s + j], 4)
                found = jnp.where(owner == r, j, found)
            order[r] = found
            place = jnp.int32(0)
            for j in range(16):
                slot = table[16 * r + j]
                mine = lax.shift_right_logical(slot, 4) == s
                place = jnp.where(mine, slot & 15, place)
            slot_of[r] = place
            return carry

        lax.fori_loop(0, 16, owned, 0)

        def placed(slot, carry):
            found = jnp.int32(0)
            for j in range(16):
                found = jnp.where(slot_of[j] == slot, j, found)
            source[slot] = found
            return carry

        lax.fori_loop(0, 16, placed, 0)

    page_order()

    loads[0].wait()
    for turn, q in enumerate(turns):
        loads[1 + turn].wait()
        if turn < 2:
            loads[5 + turn].start()
        rows = quarter(q)
        local = tok[rows, :].astype(F32)
        norm = jnp.sum(local * local, axis=1, keepdims=True)
        part = (local * gain[...]).astype(BF16)
        scaled[rows, :] = part
        kvp[q, 0:QUARTER, :] = jnp.dot(part, kvw[...], preferred_element_type=F32)
        turned = jnp.transpose(jnp.broadcast_to(norm, (QUARTER, QUARTER)))
        kvp[q, QUARTER:QUARTER + 8, :] = turned[0:8, :]
        if turn == 0:
            pl.semaphore_wait(barrier, len(near))
        if turn < 3:
            send(kvp.at[q], kvr.at[n], a_send.at[turn], a_recv.at[n], (s, w, q))

    def pass_on(first):
        if first != 1:
            pl.semaphore_wait(up_sem, 1)
            pl.semaphore_wait(down_sem, 1)
        if first < 2:
            pl.semaphore_signal(up_sem, inc=1, device_id=z_prev, device_id_type=MESH)
            pl.semaphore_signal(down_sem, inc=1, device_id=z_next, device_id_type=MESH)

    pass_on(1)

    loads[5].wait()
    for j in range(2):
        q = 2 * j + 1 - k
        rows = pl.ds(pl.multiple_of(q * QUARTER, QUARTER), QUARTER)
        qs1[j] = jnp.dot(scaled[rows, :], qw[...], preferred_element_type=F32).astype(BF16)
    send(qs1, qr1, q_send.at[0], q_recv.at[0], partner)

    index = (
        s * BLOCK + n * QUARTER
        + lax.broadcasted_iota(jnp.int32, (QUARTER, HD), 0)
    )
    end0 = lens[0]
    end1 = end0 + lens[1]
    end2 = end1 + lens[2]
    begin = jnp.where(index >= end0, end0, 0)
    begin = jnp.where(index >= end1, end1, begin)
    begin = jnp.where(index >= end2, end2, begin)
    angle = (index - begin).astype(F32) * freq[...]
    lane = lax.broadcasted_iota(jnp.int32, (QUARTER, HD), 1)
    cos_s[...] = jnp.cos(angle)
    sine = jnp.sin(angle)
    sin_s[...] = jnp.where(lane < HD // 2, -sine, sine)

    for step in (1, 2, 3):
        q = lax.rem(n + step, 4)
        arrived(kvr.at[q], a_recv.at[q])
    total = kvp[n] + kvr[lax.rem(n + 1, 4)] + kvr[lax.rem(n + 2, 4)] + kvr[lax.rem(n + 3, 4)]
    rinv = lax.rsqrt(total[QUARTER:QUARTER + 1, :] / WIDTH + EPS)
    rinv = jnp.transpose(jnp.broadcast_to(rinv, (QUARTER, QUARTER)))
    rinv_s[...] = rinv

    def rotate(values):
        return values * cos_s[...] + pltpu.roll(values, HD // 2, 1) * sin_s[...]

    plain = total[0:QUARTER, :] * rinv
    final = jnp.where(w < KV_HEADS, rotate(plain), plain).astype(BF16)
    mykv[...] = final
    pages[pl.ds(4 * n, 4)] = final.reshape(4, 32, HD)

    unit = unit_y(0, k)
    send(
        mykv, kv_all.at[0, 4 * home_half + n], b_send,
        kv_recv.at[0, 4 * home_half + n], (s, home, n),
    )

    for j in range(2):
        q = 2 * j + k
        rows = pl.ds(pl.multiple_of(q * QUARTER, QUARTER), QUARTER)
        qf[j] = jnp.dot(scaled[rows, :], qw[...], preferred_element_type=F32)
    arrived(qr1, q_recv.at[0])
    qs2[...] = (qf[1 - yl] + qr1[1 - yl].astype(F32)).astype(BF16)
    send(qs2, qr2, q_send.at[1], q_recv.at[1], across)


    straight = (7, 8)
    hops = {0: (1, 3), 1: (1,), 3: (1, 3), 4: (1,), 6: (1,), 7: (1,)}

    def piece_copy(block, action):
        step, target = ((0, at_y(1)), (0, at_y(3)), (0, partner), (None, at_y(1 + 2 * k)),
                        (1, partner), (3, partner), (2, partner), (0, y_far))[action]
        piece = unit_y(3 + 2 * k if step is None else step, k)
        return pltpu.make_async_remote_copy(
            src_ref=kv_all.at[block, piece], dst_ref=kv_all.at[block, piece],
            send_sem=kv_send.at[block, min(action, 3) if action == 7 else action], recv_sem=kv_recv.at[block, piece],
            device_id=target, device_id_type=MESH,
        )

    def jump_copy(block, step):
        return pltpu.make_async_remote_copy(
            src_ref=kv_all.at[block, unit], dst_ref=kv_all.at[block + step, unit],
            send_sem=z_send.at[block, step // 2], recv_sem=kv_recv.at[block + step, unit],
            device_id=(lax.rem(s + step, 16), w, n), device_id_type=MESH,
        )

    def spread(block, *actions):
        for action in actions:
            piece_copy(block, action).start()

    def landed(block, piece):
        arrived(kv_all.at[block, piece], kv_recv.at[block, piece])

    def own_unit(block):
        landed(block, unit)
        for step in hops.get(block, ()):
            pl.when(s < 16 - step)(lambda step=step: jump_copy(block, step).start())
        spread(block, 0, 1, 2)
        if block in straight:
            spread(block, 7)

    def near_units(block):
        landed(block, unit_y(1, k))
        landed(block, unit_y(3, k))
        spread(block, *((4, 5) if block in straight else (3, 4, 5)))

    def far_unit(block):
        landed(block, unit_y(2, k))
        spread(block, 6)

    def settle(block):
        for step in hops.get(block, ()):
            pl.when(s < 16 - step)(lambda step=step: jump_copy(block, step).wait_send())
        for action in (0, 1, 2, 7 if block in straight else 3, 4, 5, 6):
            piece_copy(block, action).wait_send()

    def present(block, action):
        if block == 0:
            action(0)
        else:
            pl.when(s >= block)(lambda: action(block))

    scale = 1.0 / (HD ** 0.5 * float(np.log(2.0)))

    def attend(block):
        for step in range(4):
            landed(block, unit_y(step, 1 - k))
        keys = kv_all[block, pl.ds(4 * key_half(x), 4)].reshape(BLOCK, HD)
        values = kv_all[block, pl.ds(4 - 4 * key_half(x), 4)].reshape(BLOCK, HD)
        shape = (4, QUARTER, BLOCK)
        key_index = (s - block) * BLOCK + lax.broadcasted_iota(jnp.int32, shape, 2)
        row = s * BLOCK + n * QUARTER + lax.broadcasted_iota(jnp.int32, (4, QUARTER, 1), 1)
        first = jnp.where(row >= end0, end0, 0)
        first = jnp.where(row >= end1, end1, first)
        first = jnp.where(row >= end2, end2, first)
        allowed = key_index >= first
        if block == 0:
            allowed = allowed & (key_index <= row)
        scores = lax.dot_general(
            queries[...], keys, (((1,), (1,)), ((), ())), preferred_element_type=F32
        )
        masked = jnp.where(allowed.reshape(BLOCK, BLOCK), scores, NEG)
        top = jnp.broadcast_to(jnp.max(masked, axis=1, keepdims=True), (BLOCK, HD))
        if block > 0:
            old = m_s[...]
            top = jnp.maximum(old, top)
        weights = jnp.exp2((masked - jnp.concatenate([top] * 4, axis=1)) * scale)
        lanes = (weights[:, 0:HD] + weights[:, HD:2 * HD]) + (
            weights[:, 2 * HD:3 * HD] + weights[:, 3 * HD:]
        )
        mixed = jnp.dot(weights.astype(BF16), values, preferred_element_type=F32)
        if block > 0:
            alpha = jnp.exp2((old - top) * scale)
            lanes = l_s[...] * alpha + lanes
            mixed = acc_s[...] * alpha + mixed
        m_s[...] = top
        l_s[...] = lanes
        acc_s[...] = mixed

    def finish_queries():
        arrived(qr2, q_recv.at[1])
        summed = qf[yl] + qr1[yl].astype(F32) + qr2[...].astype(F32)
        for h in range(4):
            value = summed[:, h * HD:(h + 1) * HD] * rinv_s[...]
            queries[h * QUARTER:(h + 1) * QUARTER, :] = rotate(value).astype(BF16)

    def gather_pages():
        for step in (1, 2, 3):
            send(
                pages.at[pl.ds(4 * n, 4)], pages.at[pl.ds(4 * n, 4)],
                pg_send.at[step - 1], pg_recv.at[n], (s, w, lax.rem(n + step, 4)),
            )

    def pack_pages():
        for step in (1, 2, 3):
            q = lax.rem(n + step, 4)
            arrived(pages.at[pl.ds(4 * q, 4)], pg_recv.at[q])
        for r in range(16):
            outg[r] = pages[order[r]]
        inc[s] = outg[s]

    def send_pages():
        for step in (8, 7, 9, 6, 10, 5, 11, 4, 12, 3, 13, 2, 14, 1, 15):
            r = lax.rem(s + step, 16)
            send(outg.at[r], inc.at[s], ex_send.at[step - 1], ex_recv.at[s], (r, w, n))

    reach = {0: 0.0, 1: 2.4, 2: 4.8, 3: 3.9, 4: 6.3, 5: 8.7, 6: 7.8, 7: 10.2, 8: 12.6}
    events = [(6.7, 0, finish_queries, None), (7.0, 0, gather_pages, None),
              (12.9, 0, pack_pages, None), (13.0, 0, send_pages, None)]
    for level in range(8):
        events.append((2.0 + 1.4 * level, 1, pass_on, 0 if level < 7 else 2))
    for block, time in reach.items():
        events.append((time, 2, own_unit, block))
        events.append((time + 2.6, 3, near_units, block))
        soon = 1.6 if block in straight else 0.0
        events.append((time + 5.2 - soon, 4, far_unit, block))
        events.append((time + 6.8 - soon, 5, attend, block))
    for _, kind, action, value in sorted(events, key=lambda e: e[:2]):
        if kind == 0:
            action()
        elif kind == 1:
            action(value)
        else:
            present(value, action)

    mixed = acc_s[...] / jnp.sum(l_s[...], axis=1, keepdims=True)
    for h in range(4):
        att[n, :, h * HD:(h + 1) * HD] = mixed[h * QUARTER:(h + 1) * QUARTER].astype(BF16)
    halves = (pl.ds(0, 64), pl.ds(64, 64))

    def share(q, part, number, device):
        piece = att.at[q, halves[part], :]
        send(piece, piece, att_send.at[number + part], att_recv.at[q, part], device)

    def shared(q, part):
        arrived(att.at[q, halves[part], :], att_recv.at[q, part])

    for part in range(2):
        share(n, part, 0, across)
    for part in range(2):
        share(n, part, 2, partner)
    loads[6].wait()
    other = 2 * (1 - yl) + k
    for part in range(2):
        shared(other, part)
        share(other, part, 4, partner)
    for q in (2 * yl + 1 - k, 2 * (1 - yl) + 1 - k):
        for part in range(2):
            shared(q, part)

    def product(step):
        return jnp.dot(att[lax.rem(x + step, 4)], ow[...], preferred_element_type=F32)

    half = WIDTH // 8
    left, right = pl.ds(0, half), pl.ds(half, half)
    starts = (64 * (1 - yh), 64 * (1 - yh) + 32, 64 * yh, 64 * yh + 32)
    chunks = [pl.ds(pl.multiple_of(start, 32), 32) for start in starts]
    routes = (
        (fxs, fxr, 0, x_next), (fxs, fxr, 1, x_prev), (gps, gpr, 1, x_next),
        (gms, gmr, 0, x_prev), (gps, gpr, 0, x_next), (gms, gmr, 1, x_prev),
    )

    def give(route, c):
        src, dst, part, device = routes[route]
        send(
            src.at[part, chunks[c], :], dst.at[part, chunks[c], :],
            o_send.at[6 * c + route], o_recv.at[6 * c + route], device,
        )

    def got(route, c):
        _, dst, part, _ = routes[route]
        arrived(dst.at[part, chunks[c], :], o_recv.at[6 * c + route])

    def relay(c):
        rows = chunks[c]
        got(0, c)
        gps[0, rows, :] = (up[rows, left] + fxr[0, rows, :].astype(F32)).astype(BF16)
        give(4, c)
        got(1, c)
        gms[1, rows, :] = (down[rows, right] + fxr[1, rows, :].astype(F32)).astype(BF16)
        give(5, c)

    def summed(c, part):
        rows = chunks[c]
        cols = pl.ds(part * half, half)
        return own[rows, cols] + gpr[part, rows, :].astype(F32) + gmr[part, rows, :].astype(F32)

    def pair(c):
        rows = pl.ds(32 * c, 32)
        for route in (2, 3, 4, 5):
            got(route, c)
        for part in range(2):
            hss[part, rows, :] = summed(c, part).astype(BF16)
            send(
                hss.at[part, rows, :], hsr.at[part, rows, :],
                o_send.at[24 + 2 * c + part], o_recv.at[24 + 2 * c + part], y_far,
            )

    far = product(2)
    fxs[0] = far[:, 0:half].astype(BF16)
    fxs[1] = far[:, half:].astype(BF16)
    give(0, 0)
    give(1, 0)
    up[...] = product(1)
    gps[1] = up[:, right].astype(BF16)
    give(2, 0)
    down[...] = product(3)
    gms[0] = down[:, left].astype(BF16)
    give(3, 0)
    give(0, 1)
    give(1, 1)
    own[...] = product(0)
    relay(0)
    give(2, 1)
    give(3, 1)
    give(0, 2)
    give(1, 2)
    relay(1)
    give(2, 2)
    give(3, 2)
    give(0, 3)
    give(1, 3)
    pair(0)
    relay(2)
    give(2, 3)
    give(3, 3)
    pair(1)
    relay(3)

    for step in range(1, 16):
        r = lax.rem(s + step, 16)
        arrived(inc.at[r], ex_recv.at[r])
    for slot in range(16):
        cache[slot] = inc[source[slot]]

    for c in range(2):
        for route in (2, 3, 4, 5):
            got(route, 2 + c)
        place = pl.ds(pl.multiple_of(64 * w + 32 * c, 32), 32)
        rows = pl.ds(32 * c, 32)
        for part in range(2):
            cols = pl.ds(part * half, half)
            base = tok[place, cols].astype(F32) + summed(2 + c, part)
            arrived(hsr.at[part, rows, :], o_recv.at[24 + 2 * c + part])
            hid[rows, cols] = (base + hsr[part, rows, :].astype(F32)).astype(BF16)

    for copy in pending:
        copy.wait_send()
    for block in range(BACK + 1):
        present(block, settle)


def on_device(tokens, norm_gain, q_weight, kv_weight, out_weight, lengths, page_table, freq):
    vmem = pl.BlockSpec(memory_space=pltpu.VMEM)
    smem = pl.BlockSpec(memory_space=pltpu.SMEM)
    hbm = pl.BlockSpec(memory_space=pl.ANY)
    dma = pltpu.SemaphoreType.DMA
    part = WIDTH // 4
    half = part // 2
    return pl.pallas_call(
        kernel,
        out_shape=(
            pltpu.VMEM((64, part), BF16),
            pltpu.VMEM((16, 32, HD), BF16),
        ),
        in_specs=[smem, smem, vmem, vmem, hbm, hbm, hbm, hbm],
        out_specs=(vmem, vmem),
        scratch_shapes=[
            pltpu.VMEM((BLOCK, part), BF16),
            pltpu.VMEM((part, HD), BF16),
            pltpu.VMEM((part, BLOCK), BF16),
            pltpu.VMEM((BLOCK, part), BF16),
            pltpu.VMEM((BLOCK, part), BF16),
            pltpu.VMEM((4, QUARTER + 8, HD), F32),
            pltpu.VMEM((4, QUARTER + 8, HD), F32),
            pltpu.VMEM((2, QUARTER, BLOCK), F32),
            pltpu.VMEM((2, QUARTER, BLOCK), BF16),
            pltpu.VMEM((2, QUARTER, BLOCK), BF16),
            pltpu.VMEM((QUARTER, BLOCK), BF16),
            pltpu.VMEM((QUARTER, BLOCK), BF16),
            pltpu.VMEM((QUARTER, HD), BF16),
            pltpu.VMEM((BACK + 1, 8, QUARTER, HD), BF16),
            pltpu.VMEM((BLOCK, HD), BF16),
            pltpu.VMEM((BLOCK, HD), F32),
            pltpu.VMEM((BLOCK, HD), F32),
            pltpu.VMEM((BLOCK, HD), F32),
            pltpu.VMEM((QUARTER, HD), F32),
            pltpu.VMEM((QUARTER, HD), F32),
            pltpu.VMEM((QUARTER, HD), F32),
            pltpu.VMEM((16, 32, HD), BF16),
            pltpu.VMEM((16, 32, HD), BF16),
            pltpu.VMEM((16, 32, HD), BF16),
            pltpu.VMEM((4, QUARTER, BLOCK), BF16),
            pltpu.VMEM((2, QUARTER, half), BF16),
            pltpu.VMEM((2, QUARTER, half), BF16),
            pltpu.VMEM((2, QUARTER, half), BF16),
            pltpu.VMEM((2, QUARTER, half), BF16),
            pltpu.VMEM((2, QUARTER, half), BF16),
            pltpu.VMEM((2, QUARTER, half), BF16),
            pltpu.VMEM((QUARTER, part), F32),
            pltpu.VMEM((QUARTER, part), F32),
            pltpu.VMEM((QUARTER, part), F32),
            pltpu.VMEM((2, 64, half), BF16),
            pltpu.VMEM((2, 64, half), BF16),
            pltpu.SMEM((16,), jnp.int32),
            pltpu.SMEM((16,), jnp.int32),
            pltpu.SMEM((16,), jnp.int32),
            dma((7,)),
            dma((3,)),
            dma((4,)),
            dma((2,)),
            dma((2,)),
            dma((BACK + 1, 7)),
            dma((BACK + 1, 8)),
            dma((BACK, 2)),
            dma,
            dma((3,)),
            dma((4,)),
            dma((15,)),
            dma((16,)),
            dma((6,)),
            dma((4, 2)),
            dma((28,)),
            dma((28,)),
            pltpu.SemaphoreType.REGULAR,
            pltpu.SemaphoreType.REGULAR,
        ],
        compiler_params=pltpu.CompilerParams(collective_id=0, has_side_effects=True),
    )(lengths, page_table, norm_gain[None, :], freq, tokens, kv_weight, q_weight, out_weight)


def solution(mesh):
    half = HD // 2
    power = THETA ** (-np.arange(half, dtype=np.float64) * 2.0 / HD)
    freq = np.concatenate([power, power]).astype(np.float32)[None, :]
    placed = (
        P("seq", "narrow"),
        P("narrow"),
        P("narrow", "wide"),
        P("narrow", "wide"),
        P("wide", "narrow"),
        P(),
        P(),
    )

    def local(*args):
        return on_device(*args, jnp.asarray(freq))

    return jax.shard_map(
        local,
        mesh=mesh,
        in_specs=placed,
        out_specs=(P(("seq", "wide"), "narrow"), P("seq", None, "wide")),
        check_vma=False,
    )
```

```python
import jax
import jax.numpy as jnp
import numpy as np
from jax import lax
from jax.experimental import pallas as pl
from jax.experimental.pallas import tpu as pltpu
from jax.sharding import PartitionSpec as P

HEADS = 32
KV_HEADS = 4
HD = 128
WIDTH = 4096
BLOCK = 512
QUARTER = 128
EPS = 1e-05
THETA = 5000000.0
NEG = -1e30
BACK = 8
MESH = pl.DeviceIdType.MESH
F32 = jnp.float32
BF16 = jnp.bfloat16


def kernel(
    lens, table, gain, freq, tok_any, kvw_any, qw_any, ow_any,
    hid, cache,
    tok, kvw, qw, ow, scaled, kvp, kvr, qf, qs1, qr1, qs2, qr2, mykv,
    kv_all, queries, m_s, l_s, acc_s, cos_s, sin_s, rinv_s, pages, outg, inc,
    att, fxs, fxr, gps, gpr, gms, gmr, up, down, own, hss, hsr, order, slot_of, source,
    in_sem, a_send, a_recv, q_send, q_recv, kv_send, kv_recv, z_send, b_send,
    pg_send, pg_recv, ex_send, ex_recv, att_send, att_recv, o_send, o_recv, up_sem, down_sem,
):
    s = lax.axis_index("seq")
    w = lax.axis_index("wide")
    n = lax.axis_index("narrow")
    x, yh = lax.div(w, 2), lax.rem(w, 2)
    yl, k = lax.div(n, 2), lax.rem(n, 2)
    y = 2 * yh + yl

    def at_y(step):
        other = lax.rem(y + step, 4)
        return (s, 2 * x + lax.div(other, 2), 2 * lax.rem(other, 2) + k)

    def unit_y(step, core):
        return 2 * lax.rem(y + step, 4) + core

    partner = (s, w, 2 * yl + 1 - k)
    across = (s, w, 2 * (1 - yl) + k)

    def key_half(column):
        return lax.rem(lax.div(column + 1, 2) + 1, 2)

    home_half = lax.rem(key_half(lax.rem(w, 4)) + lax.div(w, 4), 2)
    home = 2 * lax.rem(w, 4) + home_half
    from_home = x + 4 * lax.rem(yh + key_half(x), 2)
    z_next = (lax.rem(s + 1, 16), w, n)
    z_prev = (lax.rem(s + 15, 16), w, n)
    z_jump = (lax.rem(s + 3, 16), w, n)
    z_back = (lax.rem(s + 13, 16), w, n)
    x_next = (s, 2 * lax.rem(x + 1, 4) + yh, n)
    x_prev = (s, 2 * lax.rem(x + 3, 4) + yh, n)
    y_far = (s, 2 * x + 1 - yh, n)

    def send(src, dst, send_sem, recv_sem, device):
        copy = pltpu.make_async_remote_copy(
            src_ref=src, dst_ref=dst, send_sem=send_sem, recv_sem=recv_sem,
            device_id=device, device_id_type=MESH,
        )
        copy.start()
        pending.append(copy)

    def arrived(dst, recv_sem):
        pltpu.make_async_remote_copy(
            src_ref=dst, dst_ref=dst, send_sem=q_send.at[0], recv_sem=recv_sem,
            device_id=partner, device_id_type=MESH,
        ).wait_recv()

    pending = []

    def quarter(q):
        return pl.ds(pl.multiple_of(q * QUARTER, QUARTER), QUARTER)

    turns = (lax.rem(n + 2, 4), 3 - n, 2 * yl + 1 - k, n)
    loads = []
    for number, (src, dst) in enumerate(
        [(kvw_any, kvw)]
        + [(tok_any.at[quarter(q), :], tok.at[quarter(q), :]) for q in turns]
        + [(qw_any, qw), (ow_any, ow)]
    ):
        load = pltpu.make_async_copy(src, dst, in_sem.at[number])
        loads.append(load)
    for load in loads[:5]:
        load.start()

    barrier = pltpu.get_barrier_semaphore()
    near = (
        [(s, w, lax.rem(n + step, 4)) for step in (1, 2, 3)]
        + [(s, home, n), (s, from_home, n), z_next, z_prev, z_jump, z_back, at_y(1), at_y(3), x_next, x_prev, y_far]
    )
    for device in near:
        pl.semaphore_signal(barrier, inc=1, device_id=device, device_id_type=MESH)

    def page_order():
        def owned(r, carry):
            found = jnp.int32(0)
            for j in range(16):
                owner = lax.shift_right_logical(table[16 * s + j], 4)
                found = jnp.where(owner == r, j, found)
            order[r] = found
            place = jnp.int32(0)
            for j in range(16):
                slot = table[16 * r + j]
                mine = lax.shift_right_logical(slot, 4) == s
                place = jnp.where(mine, slot & 15, place)
            slot_of[r] = place
            return carry

        lax.fori_loop(0, 16, owned, 0)

        def placed(slot, carry):
            found = jnp.int32(0)
            for j in range(16):
                found = jnp.where(slot_of[j] == slot, j, found)
            source[slot] = found
            return carry

        lax.fori_loop(0, 16, placed, 0)

    page_order()

    loads[0].wait()
    for turn, q in enumerate(turns):
        loads[1 + turn].wait()
        if turn < 2:
            loads[5 + turn].start()
        rows = quarter(q)
        local = tok[rows, :].astype(F32)
        norm = jnp.sum(local * local, axis=1, keepdims=True)
        part = (local * gain[...]).astype(BF16)
        scaled[rows, :] = part
        kvp[q, 0:QUARTER, :] = jnp.dot(part, kvw[...], preferred_element_type=F32)
        turned = jnp.transpose(jnp.broadcast_to(norm, (QUARTER, QUARTER)))
        kvp[q, QUARTER:QUARTER + 8, :] = turned[0:8, :]
        if turn == 0:
            pl.semaphore_wait(barrier, len(near))
        if turn < 3:
            send(kvp.at[q], kvr.at[n], a_send.at[turn], a_recv.at[n], (s, w, q))

    def pass_on(first):
        if first != 1:
            pl.semaphore_wait(up_sem, 1)
            pl.semaphore_wait(down_sem, 1)
        if first < 2:
            pl.semaphore_signal(up_sem, inc=1, device_id=z_prev, device_id_type=MESH)
            pl.semaphore_signal(down_sem, inc=1, device_id=z_next, device_id_type=MESH)

    pass_on(1)

    loads[5].wait()
    for j in range(2):
        q = 2 * j + 1 - k
        rows = pl.ds(pl.multiple_of(q * QUARTER, QUARTER), QUARTER)
        qs1[j] = jnp.dot(scaled[rows, :], qw[...], preferred_element_type=F32).astype(BF16)
    send(qs1, qr1, q_send.at[0], q_recv.at[0], partner)

    index = (
        s * BLOCK + n * QUARTER
        + lax.broadcasted_iota(jnp.int32, (QUARTER, HD), 0)
    )
    end0 = lens[0]
    end1 = end0 + lens[1]
    end2 = end1 + lens[2]
    begin = jnp.where(index >= end0, end0, 0)
    begin = jnp.where(index >= end1, end1, begin)
    begin = jnp.where(index >= end2, end2, begin)
    angle = (index - begin).astype(F32) * freq[...]
    lane = lax.broadcasted_iota(jnp.int32, (QUARTER, HD), 1)
    cos_s[...] = jnp.cos(angle)
    sine = jnp.sin(angle)
    sin_s[...] = jnp.where(lane < HD // 2, -sine, sine)

    for step in (1, 2, 3):
        q = lax.rem(n + step, 4)
        arrived(kvr.at[q], a_recv.at[q])
    total = kvp[n] + kvr[lax.rem(n + 1, 4)] + kvr[lax.rem(n + 2, 4)] + kvr[lax.rem(n + 3, 4)]
    rinv = lax.rsqrt(total[QUARTER:QUARTER + 1, :] / WIDTH + EPS)
    rinv = jnp.transpose(jnp.broadcast_to(rinv, (QUARTER, QUARTER)))
    rinv_s[...] = rinv

    def rotate(values):
        return values * cos_s[...] + pltpu.roll(values, HD // 2, 1) * sin_s[...]

    plain = total[0:QUARTER, :] * rinv
    final = jnp.where(w < KV_HEADS, rotate(plain), plain).astype(BF16)
    mykv[...] = final
    pages[pl.ds(4 * n, 4)] = final.reshape(4, 32, HD)

    unit = unit_y(0, k)
    send(
        mykv, kv_all.at[0, 4 * home_half + n], b_send,
        kv_recv.at[0, 4 * home_half + n], (s, home, n),
    )

    for j in range(2):
        q = 2 * j + k
        rows = pl.ds(pl.multiple_of(q * QUARTER, QUARTER), QUARTER)
        qf[j] = jnp.dot(scaled[rows, :], qw[...], preferred_element_type=F32)
    arrived(qr1, q_recv.at[0])
    qs2[...] = (qf[1 - yl] + qr1[1 - yl].astype(F32)).astype(BF16)
    send(qs2, qr2, q_send.at[1], q_recv.at[1], across)


    straight = (7, 8)
    hops = {0: (1, 3), 1: (1,), 3: (1, 3), 4: (1,), 6: (1,), 7: (1,)}

    def piece_copy(block, action):
        step, target = ((0, at_y(1)), (0, at_y(3)), (0, partner), (None, at_y(1 + 2 * k)),
                        (1, partner), (3, partner), (2, partner), (0, y_far))[action]
        piece = unit_y(3 + 2 * k if step is None else step, k)
        return pltpu.make_async_remote_copy(
            src_ref=kv_all.at[block, piece], dst_ref=kv_all.at[block, piece],
            send_sem=kv_send.at[block, min(action, 3) if action == 7 else action], recv_sem=kv_recv.at[block, piece],
            device_id=target, device_id_type=MESH,
        )

    def jump_copy(block, step):
        return pltpu.make_async_remote_copy(
            src_ref=kv_all.at[block, unit], dst_ref=kv_all.at[block + step, unit],
            send_sem=z_send.at[block, step // 2], recv_sem=kv_recv.at[block + step, unit],
            device_id=(lax.rem(s + step, 16), w, n), device_id_type=MESH,
        )

    def spread(block, *actions):
        for action in actions:
            piece_copy(block, action).start()

    def landed(block, piece):
        arrived(kv_all.at[block, piece], kv_recv.at[block, piece])

    def own_unit(block):
        landed(block, unit)
        for step in hops.get(block, ()):
            pl.when(s < 16 - step)(lambda step=step: jump_copy(block, step).start())
        spread(block, 0, 1, 2)
        if block in straight:
            spread(block, 7)

    def near_units(block):
        landed(block, unit_y(1, k))
        landed(block, unit_y(3, k))
        spread(block, *((4, 5) if block in straight else (3, 4, 5)))

    def far_unit(block):
        landed(block, unit_y(2, k))
        spread(block, 6)

    def settle(block):
        for step in hops.get(block, ()):
            pl.when(s < 16 - step)(lambda step=step: jump_copy(block, step).wait_send())
        for action in (0, 1, 2, 7 if block in straight else 3, 4, 5, 6):
            piece_copy(block, action).wait_send()

    def present(block, action):
        if block == 0:
            action(0)
        else:
            pl.when(s >= block)(lambda: action(block))

    scale = 1.0 / (HD ** 0.5 * float(np.log(2.0)))

    def attend(block):
        for step in range(4):
            landed(block, unit_y(step, 1 - k))
        keys = kv_all[block, pl.ds(4 * key_half(x), 4)].reshape(BLOCK, HD)
        values = kv_all[block, pl.ds(4 - 4 * key_half(x), 4)].reshape(BLOCK, HD)
        shape = (4, QUARTER, BLOCK)
        key_index = (s - block) * BLOCK + lax.broadcasted_iota(jnp.int32, shape, 2)
        row = s * BLOCK + n * QUARTER + lax.broadcasted_iota(jnp.int32, (4, QUARTER, 1), 1)
        first = jnp.where(row >= end0, end0, 0)
        first = jnp.where(row >= end1, end1, first)
        first = jnp.where(row >= end2, end2, first)
        allowed = key_index >= first
        if block == 0:
            allowed = allowed & (key_index <= row)
        scores = lax.dot_general(
            queries[...], keys, (((1,), (1,)), ((), ())), preferred_element_type=F32
        )
        masked = jnp.where(allowed.reshape(BLOCK, BLOCK), scores, NEG)
        top = jnp.broadcast_to(jnp.max(masked, axis=1, keepdims=True), (BLOCK, HD))
        if block > 0:
            old = m_s[...]
            top = jnp.maximum(old, top)
        weights = jnp.exp2((masked - jnp.concatenate([top] * 4, axis=1)) * scale)
        lanes = (weights[:, 0:HD] + weights[:, HD:2 * HD]) + (
            weights[:, 2 * HD:3 * HD] + weights[:, 3 * HD:]
        )
        mixed = jnp.dot(weights.astype(BF16), values, preferred_element_type=F32)
        if block > 0:
            alpha = jnp.exp2((old - top) * scale)
            lanes = l_s[...] * alpha + lanes
            mixed = acc_s[...] * alpha + mixed
        m_s[...] = top
        l_s[...] = lanes
        acc_s[...] = mixed

    def finish_queries():
        arrived(qr2, q_recv.at[1])
        summed = qf[yl] + qr1[yl].astype(F32) + qr2[...].astype(F32)
        for h in range(4):
            value = summed[:, h * HD:(h + 1) * HD] * rinv_s[...]
            queries[h * QUARTER:(h + 1) * QUARTER, :] = rotate(value).astype(BF16)

    def gather_pages():
        for step in (1, 2, 3):
            send(
                pages.at[pl.ds(4 * n, 4)], pages.at[pl.ds(4 * n, 4)],
                pg_send.at[step - 1], pg_recv.at[n], (s, w, lax.rem(n + step, 4)),
            )

    def pack_pages():
        for step in (1, 2, 3):
            q = lax.rem(n + step, 4)
            arrived(pages.at[pl.ds(4 * q, 4)], pg_recv.at[q])
        for r in range(16):
            outg[r] = pages[order[r]]
        inc[s] = outg[s]

    def send_pages():
        for step in (8, 7, 9, 6, 10, 5, 11, 4, 12, 3, 13, 2, 14, 1, 15):
            r = lax.rem(s + step, 16)
            send(outg.at[r], inc.at[s], ex_send.at[step - 1], ex_recv.at[s], (r, w, n))

    reach = {0: 0.0, 1: 2.4, 2: 4.8, 3: 3.9, 4: 6.3, 5: 8.7, 6: 7.8, 7: 10.2, 8: 12.6}
    events = [(6.7, 0, finish_queries, None), (7.0, 0, gather_pages, None),
              (12.9, 0, pack_pages, None), (13.0, 0, send_pages, None)]
    for level in range(8):
        events.append((2.0 + 1.4 * level, 1, pass_on, 0 if level < 7 else 2))
    for block, time in reach.items():
        events.append((time, 2, own_unit, block))
        events.append((time + 2.6, 3, near_units, block))
        soon = 1.6 if block in straight else 0.0
        events.append((time + 5.2 - soon, 4, far_unit, block))
        events.append((time + 6.8 - soon, 5, attend, block))
    for _, kind, action, value in sorted(events, key=lambda e: e[:2]):
        if kind == 0:
            action()
        elif kind == 1:
            action(value)
        else:
            present(value, action)

    halves = (pl.ds(0, 64), pl.ds(64, 64))

    def share(q, part, number, device):
        piece = att.at[q, halves[part], :]
        send(piece, piece, att_send.at[number + part], att_recv.at[q, part], device)

    def shared(q, part):
        arrived(att.at[q, halves[part], :], att_recv.at[q, part])

    for part in range(2):
        for h in range(4):
            rows = pl.ds(h * QUARTER + 64 * part, 64)
            mixed = acc_s[rows, :] / jnp.sum(l_s[rows, :], axis=1, keepdims=True)
            att[n, halves[part], h * HD:(h + 1) * HD] = mixed.astype(BF16)
        share(n, part, 0, across)
    for part in range(2):
        share(n, part, 2, partner)
    loads[6].wait()
    other = 2 * (1 - yl) + k
    for part in range(2):
        shared(other, part)
        share(other, part, 4, partner)
    for q in (2 * yl + 1 - k, 2 * (1 - yl) + 1 - k):
        for part in range(2):
            shared(q, part)

    def product(step):
        return jnp.dot(att[lax.rem(x + step, 4)], ow[...], preferred_element_type=F32)

    half = WIDTH // 8
    left, right = pl.ds(0, half), pl.ds(half, half)
    starts = (64 * (1 - yh), 64 * (1 - yh) + 32, 64 * yh, 64 * yh + 32)
    chunks = [pl.ds(pl.multiple_of(start, 32), 32) for start in starts]
    routes = (
        (fxs, fxr, 0, x_next), (fxs, fxr, 1, x_prev), (gps, gpr, 1, x_next),
        (gms, gmr, 0, x_prev), (gps, gpr, 0, x_next), (gms, gmr, 1, x_prev),
    )

    def give(route, c):
        src, dst, part, device = routes[route]
        send(
            src.at[part, chunks[c], :], dst.at[part, chunks[c], :],
            o_send.at[6 * c + route], o_recv.at[6 * c + route], device,
        )

    def got(route, c):
        _, dst, part, _ = routes[route]
        arrived(dst.at[part, chunks[c], :], o_recv.at[6 * c + route])

    def relay(c):
        rows = chunks[c]
        got(0, c)
        gps[0, rows, :] = (up[rows, left] + fxr[0, rows, :].astype(F32)).astype(BF16)
        give(4, c)
        got(1, c)
        gms[1, rows, :] = (down[rows, right] + fxr[1, rows, :].astype(F32)).astype(BF16)
        give(5, c)

    def summed(c, part):
        rows = chunks[c]
        cols = pl.ds(part * half, half)
        return own[rows, cols] + gpr[part, rows, :].astype(F32) + gmr[part, rows, :].astype(F32)

    def pair(c):
        rows = pl.ds(32 * c, 32)
        for route in (2, 3, 4, 5):
            got(route, c)
        for part in range(2):
            hss[part, rows, :] = summed(c, part).astype(BF16)
            send(
                hss.at[part, rows, :], hsr.at[part, rows, :],
                o_send.at[24 + 2 * c + part], o_recv.at[24 + 2 * c + part], y_far,
            )

    far = product(2)
    fxs[0] = far[:, 0:half].astype(BF16)
    fxs[1] = far[:, half:].astype(BF16)
    give(0, 0)
    give(1, 0)
    up[...] = product(1)
    gps[1] = up[:, right].astype(BF16)
    give(2, 0)
    down[...] = product(3)
    gms[0] = down[:, left].astype(BF16)
    give(3, 0)
    give(0, 1)
    give(1, 1)
    own[...] = product(0)
    relay(0)
    give(2, 1)
    give(3, 1)
    give(0, 2)
    give(1, 2)
    relay(1)
    give(2, 2)
    give(3, 2)
    give(0, 3)
    give(1, 3)
    pair(0)
    relay(2)
    give(2, 3)
    give(3, 3)
    pair(1)
    relay(3)

    for step in range(1, 16):
        r = lax.rem(s + step, 16)
        arrived(inc.at[r], ex_recv.at[r])
    for slot in range(16):
        cache[slot] = inc[source[slot]]

    for c in range(2):
        for route in (2, 3, 4, 5):
            got(route, 2 + c)
        place = pl.ds(pl.multiple_of(64 * w + 32 * c, 32), 32)
        rows = pl.ds(32 * c, 32)
        for part in range(2):
            cols = pl.ds(part * half, half)
            base = tok[place, cols].astype(F32) + summed(2 + c, part)
            arrived(hsr.at[part, rows, :], o_recv.at[24 + 2 * c + part])
            hid[rows, cols] = (base + hsr[part, rows, :].astype(F32)).astype(BF16)

    for copy in pending:
        copy.wait_send()
    for block in range(BACK + 1):
        present(block, settle)


def on_device(tokens, norm_gain, q_weight, kv_weight, out_weight, lengths, page_table, freq):
    vmem = pl.BlockSpec(memory_space=pltpu.VMEM)
    smem = pl.BlockSpec(memory_space=pltpu.SMEM)
    hbm = pl.BlockSpec(memory_space=pl.ANY)
    dma = pltpu.SemaphoreType.DMA
    part = WIDTH // 4
    half = part // 2
    return pl.pallas_call(
        kernel,
        out_shape=(
            pltpu.VMEM((64, part), BF16),
            pltpu.VMEM((16, 32, HD), BF16),
        ),
        in_specs=[smem, smem, vmem, vmem, hbm, hbm, hbm, hbm],
        out_specs=(vmem, vmem),
        scratch_shapes=[
            pltpu.VMEM((BLOCK, part), BF16),
            pltpu.VMEM((part, HD), BF16),
            pltpu.VMEM((part, BLOCK), BF16),
            pltpu.VMEM((BLOCK, part), BF16),
            pltpu.VMEM((BLOCK, part), BF16),
            pltpu.VMEM((4, QUARTER + 8, HD), F32),
            pltpu.VMEM((4, QUARTER + 8, HD), F32),
            pltpu.VMEM((2, QUARTER, BLOCK), F32),
            pltpu.VMEM((2, QUARTER, BLOCK), BF16),
            pltpu.VMEM((2, QUARTER, BLOCK), BF16),
            pltpu.VMEM((QUARTER, BLOCK), BF16),
            pltpu.VMEM((QUARTER, BLOCK), BF16),
            pltpu.VMEM((QUARTER, HD), BF16),
            pltpu.VMEM((BACK + 1, 8, QUARTER, HD), BF16),
            pltpu.VMEM((BLOCK, HD), BF16),
            pltpu.VMEM((BLOCK, HD), F32),
            pltpu.VMEM((BLOCK, HD), F32),
            pltpu.VMEM((BLOCK, HD), F32),
            pltpu.VMEM((QUARTER, HD), F32),
            pltpu.VMEM((QUARTER, HD), F32),
            pltpu.VMEM((QUARTER, HD), F32),
            pltpu.VMEM((16, 32, HD), BF16),
            pltpu.VMEM((16, 32, HD), BF16),
            pltpu.VMEM((16, 32, HD), BF16),
            pltpu.VMEM((4, QUARTER, BLOCK), BF16),
            pltpu.VMEM((2, QUARTER, half), BF16),
            pltpu.VMEM((2, QUARTER, half), BF16),
            pltpu.VMEM((2, QUARTER, half), BF16),
            pltpu.VMEM((2, QUARTER, half), BF16),
            pltpu.VMEM((2, QUARTER, half), BF16),
            pltpu.VMEM((2, QUARTER, half), BF16),
            pltpu.VMEM((QUARTER, part), F32),
            pltpu.VMEM((QUARTER, part), F32),
            pltpu.VMEM((QUARTER, part), F32),
            pltpu.VMEM((2, 64, half), BF16),
            pltpu.VMEM((2, 64, half), BF16),
            pltpu.SMEM((16,), jnp.int32),
            pltpu.SMEM((16,), jnp.int32),
            pltpu.SMEM((16,), jnp.int32),
            dma((7,)),
            dma((3,)),
            dma((4,)),
            dma((2,)),
            dma((2,)),
            dma((BACK + 1, 7)),
            dma((BACK + 1, 8)),
            dma((BACK, 2)),
            dma,
            dma((3,)),
            dma((4,)),
            dma((15,)),
            dma((16,)),
            dma((6,)),
            dma((4, 2)),
            dma((28,)),
            dma((28,)),
            pltpu.SemaphoreType.REGULAR,
            pltpu.SemaphoreType.REGULAR,
        ],
        compiler_params=pltpu.CompilerParams(collective_id=0, has_side_effects=True),
    )(lengths, page_table, norm_gain[None, :], freq, tokens, kv_weight, q_weight, out_weight)


def solution(mesh):
    half = HD // 2
    power = THETA ** (-np.arange(half, dtype=np.float64) * 2.0 / HD)
    freq = np.concatenate([power, power]).astype(np.float32)[None, :]
    placed = (
        P("seq", "narrow"),
        P("narrow"),
        P("narrow", "wide"),
        P("narrow", "wide"),
        P("wide", "narrow"),
        P(),
        P(),
    )

    def local(*args):
        return on_device(*args, jnp.asarray(freq))

    return jax.shard_map(
        local,
        mesh=mesh,
        in_specs=placed,
        out_specs=(P(("seq", "wide"), "narrow"), P("seq", None, "wide")),
        check_vma=False,
    )
```
